32 devices in a mesh: row: 8 (over y, x, core), rep: 4 (over z).
Axes of the slice: x: 2, y: 2, z: 4, core: 2. Of those that a mesh axis runs over, the one named last changes fastest.
Arguments:
- features: bfloat16 [8192, 256], P('row'), may hold values from -6 to 6
- weight_self: bfloat16 [256, 256], replicated, may hold values from -0.375 to 0.375
- weight_neigh: bfloat16 [256, 256], replicated, may hold values from -0.375 to 0.375
- degrees: int32 [8192], P('row'), may hold values from 1 to 47
- tile_values: bfloat16 [8, 8, 48, 128, 128], P('row', 'rep'), may hold values from 0 to 1
- tile_blocks: int32 [8, 8, 48, 2], P('row', 'rep'), may hold values from 0 to 7
- tile_count: int32 [8, 8], P('row', 'rep'), may hold values from 1 to 48, as said below
- cotangent: bfloat16 [8192, 256], P(('row', 'rep')), may hold values from -6 to 6
Outputs:
- output: bfloat16 [8192, 256], P(('row', 'rep'))
- grad_self: float32 [256, 256], replicated
- grad_neigh: float32 [256, 256], replicated
- grad_features: bfloat16 [8192, 256], P(('row', 'rep'))
The draws below stay inside these ranges and needn't reach their ends.
Inputs may be any that keep to these rules, and one draw needn't show every extreme that they name: `tile_count`: for some row index and section all 48 slots are live in every draw.
All inputs are finite; a program needn't handle non-finite values.
Results may differ from the reference program's by a relative error of at most 0.024.
Values may be sent and summed in bfloat16 or wider, within the bound.
A program may use at most 64 MiB of HBM per device.

```python
import jax
import jax.numpy as jnp
from jax import lax

FEAT = 256
HID = 256
TILE = 128
BLK_DEV = 8
TCAP = 48
NODES_DEV = 1024
NODES = 8192
SECTIONS = 8


def draw_tile_count(key, part):
    base = jax.random.randint(jax.random.fold_in(key, 11), (SECTIONS, SECTIONS), 1, TCAP // 4 + 1)
    section_load = jax.random.randint(jax.random.fold_in(key, 12), (1, SECTIONS), 1, 5)
    count = jnp.minimum(base * section_load, TCAP)
    return count.at[0, 0].set(TCAP).astype(jnp.int32)


def touch_ends(result, key, low, largest):
    index_at = [jax.random.randint(jax.random.fold_in(key, axis), (), 0, length) for axis, length in enumerate(result.shape)]
    widest = result.shape.index(max(result.shape))
    next_to = index_at[:widest] + [(index_at[widest] + 1) % result.shape[widest]] + index_at[widest + 1:]
    return result.at[tuple(index_at)].set(low).at[tuple(next_to)].set(largest)


def block_levels(stream_key, dims, pieces, smallest, high):
    factor_of = 1.0
    for axis_at, shards_of in pieces:
        draws = jax.random.uniform(jax.random.fold_in(jax.random.fold_in(stream_key, 6), axis_at), (shards_of,), jnp.float32, smallest / len(pieces), high / len(pieces))
        factor_of = factor_of * jnp.repeat(jnp.exp(draws), dims[axis_at] // shards_of).reshape((-1,) + (1,) * (len(dims) - 1 - axis_at))
    return factor_of


def scatter_about(key, shape, width, most, cuts=(), dtype=jnp.bfloat16):
    drawn = jax.random.normal(key, shape, jnp.float32) * width
    if len(cuts) > 0:
        drawn = block_levels(key, shape, cuts, -0.22, 0.18) * drawn
    return jnp.clip(drawn, min=-most, max=most).astype(dtype)


def setup_inputs(seed: int = 0) -> dict:
    seeds = jax.random.split(jax.random.key(seed), 9)
    return {
        "features": scatter_about(seeds[0], (NODES, FEAT), 1.0, 6.0, ((0, 8),)),
        "weight_self": scatter_about(seeds[1], (FEAT, HID), FEAT ** -0.5, 0.375),
        "weight_neigh": scatter_about(seeds[2], (FEAT, HID), FEAT ** -0.5, 0.375),
        "degrees": touch_ends(jax.random.randint(seeds[3], (NODES,), 1, 48), jax.random.fold_in(seeds[3], 1), 1, 47).astype(jnp.int32),
        "tile_values": jnp.clip(1.0 * jax.random.uniform(seeds[4], (SECTIONS, SECTIONS, TCAP, TILE, TILE), jnp.float32) ** block_levels(seeds[4], (SECTIONS, SECTIONS, TCAP, TILE, TILE), ((0, 8), (1, 4)), -0.2, 0.2), 0.0, 1.0).astype(jnp.bfloat16),
        "tile_blocks": touch_ends(jax.random.randint(seeds[5], (SECTIONS, SECTIONS, TCAP, 2), 0, BLK_DEV), jax.random.fold_in(seeds[5], 1), 0, BLK_DEV - 1).astype(jnp.int32),
        "tile_count": draw_tile_count(jax.random.fold_in(seeds[8], 71), 0),
        "cotangent": scatter_about(seeds[7], (NODES, HID), 1.0, 6.0, ((0, 32),)),
    }


def hot_tables(blocks, count):
    live = (jnp.arange(TCAP)[None, :] < count[:, None]).astype(jnp.float32)
    dest_hot = (blocks[..., 0][..., None] == jnp.arange(BLK_DEV)[None, None, :]).astype(jnp.float32) * live[..., None]
    src_hot = (blocks[..., 1][..., None] == jnp.arange(BLK_DEV)[None, None, :]).astype(jnp.float32)
    return dest_hot, src_hot


def reference(features, weight_self, weight_neigh, degrees, tile_values, tile_blocks, tile_count, cotangent):
    feat_blocks = features.astype(jnp.float32).reshape(SECTIONS, BLK_DEV, TILE, FEAT)

    def forward_row(index):
        vals = tile_values[index].astype(jnp.float32)
        dest_hot, src_hot = hot_tables(tile_blocks[index], tile_count[index])
        picked = jnp.einsum('stc,scif->stif', src_hot, feat_blocks)
        prod = jnp.einsum('stij,stjf->stif', vals, picked)
        return jnp.einsum('stb,stif->bif', dest_hot, prod).reshape(NODES_DEV, FEAT)

    agg_sum = lax.map(forward_row, jnp.arange(SECTIONS)).reshape(NODES, FEAT)
    degree = degrees.astype(jnp.float32)[:, None]
    agg = (agg_sum / degree).astype(jnp.bfloat16)
    pre = jnp.dot(features, weight_self, preferred_element_type=jnp.float32) + jnp.dot(agg, weight_neigh, preferred_element_type=jnp.float32)
    output = jax.nn.silu(pre).astype(jnp.bfloat16)
    sig = jax.nn.sigmoid(pre)
    gpre = (cotangent.astype(jnp.float32) * sig * (1.0 + pre * (1.0 - sig))).astype(jnp.bfloat16)
    grad_self = jnp.dot(features.T, gpre, preferred_element_type=jnp.float32)
    grad_neigh = jnp.dot(agg.T, gpre, preferred_element_type=jnp.float32)
    dagg = (jnp.dot(gpre, weight_neigh.T, preferred_element_type=jnp.float32) / degree).astype(jnp.bfloat16)
    dagg_blocks = dagg.astype(jnp.float32).reshape(SECTIONS, BLK_DEV, TILE, FEAT)

    def back_row(total, index):
        vals = tile_values[index].astype(jnp.float32)
        dest_hot, src_hot = hot_tables(tile_blocks[index], tile_count[index])
        picked = jnp.einsum('stb,bif->stif', dest_hot, dagg_blocks[index])
        contrib = jnp.einsum('stij,stif->stjf', vals, picked)
        return total + jnp.einsum('stc,stjf->scjf', src_hot, contrib), None

    start = jnp.zeros((SECTIONS, BLK_DEV, TILE, FEAT), jnp.float32)
    back_total, unused = lax.scan(back_row, start, jnp.arange(SECTIONS))
    back_sum = back_total.reshape(NODES, FEAT).astype(jnp.bfloat16)
    grad_features = (jnp.dot(gpre, weight_self.T, preferred_element_type=jnp.float32) + back_sum.astype(jnp.float32)).astype(jnp.bfloat16)
    return (output, grad_self, grad_neigh, grad_features)
```

```python
import functools

import jax
import jax.numpy as jnp
from jax import lax
from jax.experimental import pallas as pl
from jax.experimental.pallas import tpu as pltpu
from jax.sharding import PartitionSpec as P

MESH = pl.DeviceIdType.MESH
F32 = jnp.float32
BF16 = jnp.bfloat16
PAIR = 2
PARTS = 4


def remote(src, dst, send, recv, device):
    return pltpu.make_async_remote_copy(
        src_ref=src, dst_ref=dst, send_sem=send, recv_sem=recv, device_id=device, device_id_type=MESH
    )


def bits_of(n):
    return (n - 1).bit_length()


def xor(a, b, n):
    total = 0
    for k in range(bits_of(n)):
        w = 2**k
        total = total + ((a // w + b // w) % 2) * w
    return total


def mirror(a, n):
    total = 0
    top = bits_of(n)
    for k in range(top):
        total = total + ((a // 2**k) % 2) * 2 ** (top - 1 - k)
    return total


def layer_kernel(
    nrow, nrep, here,
    feat_hbm, wself, wneigh, deg, cot, tiles_hbm, blocks, count,
    out, wall, gfeat,
    tiles, runs, adj, keys, tab_v, tab_s, my_feat, src, mine, part, part_in, agg_all, gpre_all,
    dagg, dagg_t, terms, pair_in, summed, plane_in, back, back_in,
    wpart, wrow_in, wrep_in, base, deg_col,
    tile_sem, tab_sem, feat_sem, own_sem,
    p1s, p1r, p1ps, p1pr, bs, br, es, er, cs, cr, fs, fr, w1s, w1r, w2s, w2r, w3s, w3r,
    d0s, d0r, d1s, d1r, d2s, d2r,
):
    row, rep = lax.axis_index("row"), lax.axis_index("rep")
    rows, width = feat_hbm.shape
    lanes = src.shape[-1]
    slices = width // lanes
    share = rows // nrep
    half = nrow // PAIR
    tile = tiles.shape[-1]
    slots = tiles.shape[1]
    nblk = rows // tile
    hi, lo = row // PAIR, row % PAIR
    hx, hy = hi % PAIR, hi // PAIR
    ny = half // PAIR
    sx, sy = rep % PAIR, rep // PAIR
    is_src = hi == rep
    is_x = jnp.logical_and(hy == sy, hx != sx)
    is_y = jnp.logical_and(hx == sx, hy != sy)
    is_d = jnp.logical_and(hx != sx, hy != sy)
    partner = (hi * PAIR + (1 - lo), rep)
    my_q = xor(hi, mirror(rep, nrep), nrep)
    owner = (rep * PAIR + lo, my_q)
    giver = (xor(rep, mirror(hi, nrep), nrep) * PAIR + lo, hi)
    moves = jnp.logical_or(owner[0] != row, owner[1] != rep)

    barrier = pltpu.get_barrier_semaphore()

    def greet(device):
        pl.semaphore_signal(barrier, inc=1, device_id=device, device_id_type=MESH)

    for d in range(1, nrow):
        greet(((row + d) % nrow, rep))
    for d in range(1, nrep):
        greet((row, (rep + d) % nrep))

    @pl.when(moves)
    def _():
        greet(owner)
        greet(giver)

    def own_copy(c, k):
        return pltpu.make_async_copy(
            feat_hbm.at[pl.ds(k * share, share), pl.ds(c * lanes, lanes)],
            src.at[c, lo * nrep + k], own_sem.at[c, k],
        )

    @pl.when(is_src)
    def _():
        for c in range(slices):
            for k in range(nrep):
                own_copy(c, k).start()

    tile_copies = [
        pltpu.make_async_copy(tiles_hbm.at[j], tiles.at[j], tile_sem.at[j]) for j in range(here)
    ]
    for copy in tile_copies:
        copy.start()
    feat_copy = pltpu.make_async_copy(
        feat_hbm.at[pl.ds(pl.multiple_of(rep * share, share), share)], my_feat, feat_sem
    )
    feat_copy.start()

    side = keys.shape[-1]
    at_row = lax.broadcasted_iota(jnp.int32, (side, side), 0)
    at_col = lax.broadcasted_iota(jnp.int32, (side, side), 1)
    for j in range(here):
        keys[...] = jnp.full(keys.shape, -1, jnp.int32)
        keys[0:1, 0:slots] = blocks[j, 0:1, :] * nblk + blocks[j, 1:2, :]
        line = jnp.broadcast_to(keys[0:1, :], (side, side))
        column = line.T
        before = jnp.where(jnp.logical_and(column == line, at_row < at_col), at_row + 1, 0)
        latest = jnp.where(jnp.logical_and(column == at_col, at_row < count[j]), at_row + 1, 0)
        tab_v[2 * j : 2 * j + 1, :] = jnp.max(before, axis=0, keepdims=True)
        tab_v[2 * j + 1 : 2 * j + 2, :] = jnp.max(latest, axis=0, keepdims=True)
    tab_copy = pltpu.make_async_copy(tab_v, tab_s, tab_sem)
    tab_copy.start()
    run = deg.shape[1]
    for b in range(rows // run):
        line = jnp.broadcast_to(deg[b : b + 1, :].astype(F32), (run, run))
        deg_col[pl.ds(b * run, run), :] = line.T
    tab_copy.wait()

    pl.semaphore_wait(barrier, nrow - 1 + nrep - 1 + 2 * moves.astype(jnp.int32))

    def hop(c, k, i, h):
        at = src.at[c, lo * nrep + k]
        return remote(at, at, p1s.at[c, k, i], p1r.at[c, k], (h * PAIR + lo, rep))

    def x_peer():
        return hy * PAIR + (1 - hx)

    def y_peer(d):
        return ((hy + d) % ny) * PAIR + hx

    def to_partner(c, k):
        at = src.at[c, lo * nrep + k]
        return remote(at, at, p1ps.at[c, k], p1pr.at[c, k], partner)

    def from_partner(c, k):
        at = src.at[c, (1 - lo) * nrep + k]
        return remote(at, at, p1ps.at[c, k], p1pr.at[c, k], partner)

    first, second = list(range(nrep // 2)), list(range(nrep // 2, nrep))

    @pl.when(is_src)
    def _():
        for c in range(slices):
            for k in range(nrep):
                own_copy(c, k).wait()
            for kx, ky in zip(first + second, second + first):
                hop(c, kx, 0, x_peer()).start()
                for d in range(1, ny):
                    hop(c, ky, d, y_peer(d)).start()
            for k in range(nrep):
                to_partner(c, k).start()

    for j in range(here):
        tile_copies[j].wait()
        runs[0] = jnp.zeros((tile, tile), F32)

        def add(slot, carry):
            runs[slot + 1] = tiles[j, slot].astype(F32) + runs[tab_s[2 * j, slot]]
            return carry

        lax.fori_loop(0, slots, add, 0)

        def place(b, carry):
            for c in range(nblk):
                block = runs[tab_s[2 * j + 1, b * nblk + c]]
                adj[j, pl.ds(pl.multiple_of(b * tile, tile), tile), c * tile : (c + 1) * tile] = block.astype(BF16)
            return carry

        lax.fori_loop(0, nblk, place, 0)

    def relay(c):
        @pl.when(is_x)
        def _():
            for k in first + second:
                hop(c, k, 0, hi).wait_recv()
                if k in first:
                    for d in range(1, ny):
                        hop(c, k, d, y_peer(d)).start()
                to_partner(c, k).start()

        @pl.when(is_y)
        def _():
            for k in second + first:
                hop(c, k, 0, hi).wait_recv()
                if k in second:
                    hop(c, k, 0, x_peer()).start()
                to_partner(c, k).start()

        @pl.when(is_d)
        def _():
            for pair in zip(first, second):
                for k in pair:
                    hop(c, k, 0, hi).wait_recv()
                    to_partner(c, k).start()

        for k in range(nrep):
            from_partner(c, k).wait_recv()

    def partial(c, q):
        total = jnp.zeros((share, lanes), F32)
        for j in range(here):
            a = adj[j, pl.ds(pl.multiple_of(q * share, share), share), :]
            f = src[c, pl.ds(j * nrep, nrep)].reshape(rows, lanes)
            total = total + jnp.dot(a, f, preferred_element_type=F32)
        return total

    last = slices - 1
    step = share // PARTS

    def send_part(c, d):
        to = (rep + d) % nrep
        return remote(
            part.at[c, d - 1], part_in.at[c, d - 1], bs.at[c, d - 1], br.at[c, d - 1], (row, to)
        )

    def send_step(d, i):
        to = (rep + d) % nrep
        at = (last, d - 1, pl.ds(i * step, step))
        return remote(part.at[at], part_in.at[at], es.at[d - 1, i], er.at[d - 1, i], (row, to))

    for c in range(slices):
        relay(c)
        for d in range(1, nrep):
            part[c, d - 1] = partial(c, (rep + d) % nrep).astype(BF16)
            if c < last:
                send_part(c, d).start()
        if c == last:
            for i in range(PARTS):
                for d in range(1, nrep):
                    send_step(d, i).start()
        mine[c] = partial(c, rep)
    feat_copy.wait()
    base[...] = jnp.dot(my_feat[...], wself[...], preferred_element_type=F32)

    def send_dagg(c, d, i):
        at = (c, rep, pl.ds(i * step, step))
        return remote(
            dagg.at[at], dagg.at[at], cs.at[c, d - 1, i], cr.at[c, d - 1, i], (row, (rep + d) % nrep)
        )

    for c in range(last):
        for d in range(1, nrep):
            send_part(c, d).wait_recv()
            mine[c] = mine[c] + part_in[c, d - 1].astype(F32)
    for i in range(PARTS):
        at = pl.ds(i * step, step)
        degree = deg_col[pl.ds(pl.multiple_of(rep * share + i * step, step), step), :]
        total = mine[last, at]
        for d in range(1, nrep):
            send_step(d, i).wait_recv()
            total = total + part_in[last, d - 1, at].astype(F32)
        sums = [mine[c, at] for c in range(last)] + [total]
        agg = jnp.concatenate([(s / degree).astype(BF16) for s in sums], axis=1)
        agg_all[at] = agg
        pre = base[at] + jnp.dot(agg, wneigh[...], preferred_element_type=F32)
        sig = jax.nn.sigmoid(pre)
        gpre = (cot[at].astype(F32) * sig * (1.0 + pre * (1.0 - sig))).astype(BF16)
        gpre_all[at] = gpre
        back_t = lax.dot_general(gpre, wneigh[...], (((1,), (1,)), ((), ())), preferred_element_type=F32)
        for c in range(slices):
            dagg[c, rep, at] = (back_t[:, c * lanes : (c + 1) * lanes] / degree).astype(BF16)
        for d in range(1, nrep):
            send_dagg(0, d, i).start()
        out[at] = (pre * sig).astype(BF16)
    for c in range(1, slices):
        for i in range(PARTS):
            for d in range(1, nrep):
                send_dagg(c, d, i).start()

    gpre = gpre_all[...]
    ws = lax.dot_general(my_feat[...], gpre, (((0,), (0,)), ((), ())), preferred_element_type=F32)
    wn = lax.dot_general(agg_all[...], gpre, (((0,), (0,)), ((), ())), preferred_element_type=F32)
    piece = wpart.shape[1]
    wpart[pl.ds(0, half)] = ws.astype(BF16).reshape(half, piece, width)
    wpart[pl.ds(half, half)] = wn.astype(BF16).reshape(half, piece, width)

    def send_w1(d):
        to = (row + d) % nrow
        return remote(wpart.at[to], wrow_in.at[d - 1], w1s.at[d - 1], w1r.at[d - 1], (to, rep))

    for d in range(1, nrow):
        send_w1(d).start()
    base[...] = lax.dot_general(gpre, wself[...], (((1,), (1,)), ((), ())), preferred_element_type=F32)

    unit = max(share, 128)
    per_unit = unit // share

    def send_pair(c, q):
        return remote(
            terms.at[c, (1 - lo) * nrep + q], pair_in.at[c, q], d0s.at[c, q], d0r.at[c, q], partner
        )

    def send_plane(c, e):
        return remote(
            summed.at[c, e - 1], plane_in.at[c, e - 1], d1s.at[c, e - 1], d1r.at[c, e - 1],
            (xor(hi, e, half) * PAIR + lo, rep),
        )

    def to_owner(c):
        return remote(back.at[c], back_in.at[c], d2s.at[c], d2r.at[c], owner)

    def make_terms(c):
        for i in range(PARTS):
            for d in range(1, nrep):
                at = (c, (rep + nrep - d) % nrep, pl.ds(i * step, step))
                remote(
                    dagg.at[at], dagg.at[at], cs.at[c, d - 1, i], cr.at[c, d - 1, i], (row, rep)
                ).wait_recv()
        dagg_t[...] = dagg[c].reshape(rows, lanes).T
        for j in (1 - lo, lo):
            for u in range(rows // unit):
                t = jnp.dot(
                    dagg_t[...], adj[j, :, u * unit : (u + 1) * unit], preferred_element_type=F32
                ).astype(BF16)
                for v in range(per_unit):
                    q = u * per_unit + v
                    terms[c, j * nrep + q] = t[:, v * share : (v + 1) * share]
                    if j is not lo:
                        send_pair(c, q).start()

    def add_pair(c):
        for e in list(range(half - 1, 0, -1)) + [0]:
            q = xor(xor(hi, e, half), mirror(rep, nrep), nrep)
            send_pair(c, q).wait_recv()
            both = terms[c, lo * nrep + q].astype(F32) + pair_in[c, q].astype(F32)
            if e > 0:
                summed[c, e - 1] = both.astype(BF16)
                send_plane(c, e).start()
            else:
                back_sum[c] = both

    def add_plane(c):
        both = back_sum[c]
        for e in range(1, half):
            send_plane(c, e).wait_recv()
            both = both + plane_in[c, e - 1].astype(F32)
        back[c] = both.astype(BF16)

        @pl.when(moves)
        def _():
            to_owner(c).start()

    back_sum = {}
    for c in range(slices):
        make_terms(c)
        if c + 1 < slices:
            add_pair(c)

    wsum = wpart[row].astype(F32)
    for d in range(1, nrow):
        send_w1(d).wait_recv()
        wsum = wsum + wrow_in[d - 1].astype(F32)
    wrep_in[rep] = wsum.astype(BF16)

    def send_w2(d):
        return remote(
            wrep_in.at[rep], wrep_in.at[rep], w2s.at[d - 1], w2r.at[d - 1], (row, (rep + d) % nrep)
        )

    for d in range(1, nrep):
        send_w2(d).start()
    add_pair(slices - 1)
    for c in range(slices - 1):
        add_plane(c)

    for d in range(1, nrep):
        remote(
            wrep_in.at[rep], wrep_in.at[(rep + nrep - d) % nrep], w2s.at[d - 1], w2r.at[d - 1], (row, rep)
        ).wait_recv()
    wsum = wrep_in[0].astype(F32)
    for k in range(1, nrep):
        wsum = wsum + wrep_in[k].astype(F32)
    wall[row] = wsum.astype(BF16)

    def send_w3(d):
        return remote(
            wall.at[row], wall.at[row], w3s.at[d - 1], w3r.at[d - 1], ((row + d) % nrow, rep)
        )

    for d in range(1, nrow):
        send_w3(d).start()
    add_plane(slices - 1)
    for d in range(1, nrow):
        remote(
            wall.at[row], wall.at[(row + nrow - d) % nrow], w3s.at[d - 1], w3r.at[d - 1], (row, rep)
        ).wait_recv()

    for c in range(slices):
        cols = slice(c * lanes, (c + 1) * lanes)

        @pl.when(moves)
        def _():
            to_owner(c).wait_recv()
            gfeat[:, cols] = (base[:, cols] + back_in[c].astype(F32).T).astype(BF16)

        @pl.when(jnp.logical_not(moves))
        def _():
            gfeat[:, cols] = (base[:, cols] + back[c].astype(F32).T).astype(BF16)

    for c in range(slices):
        @pl.when(is_src)
        def _():
            for k in range(nrep):
                hop(c, k, 0, x_peer()).wait_send()
                for d in range(1, ny):
                    hop(c, k, d, y_peer(d)).wait_send()

        @pl.when(is_x)
        def _():
            for k in first:
                for d in range(1, ny):
                    hop(c, k, d, y_peer(d)).wait_send()

        @pl.when(is_y)
        def _():
            for k in second:
                hop(c, k, 0, x_peer()).wait_send()

        for k in range(nrep):
            to_partner(c, k).wait_send()
            send_pair(c, k).wait_send()
        for d in range(1, nrep):
            if c < last:
                send_part(c, d).wait_send()
            for i in range(PARTS):
                if c == last:
                    send_step(d, i).wait_send()
                send_dagg(c, d, i).wait_send()
        for e in range(1, half):
            send_plane(c, e).wait_send()

        @pl.when(moves)
        def _():
            to_owner(c).wait_send()

    for d in range(1, nrep):
        send_w2(d).wait_send()
    for d in range(1, nrow):
        send_w1(d).wait_send()
        send_w3(d).wait_send()


def close_kernel(out_in, wall, gfeat_in, out, gself, gneigh, gfeat):
    half = wall.shape[0] // 2
    out[...] = out_in[...]
    gfeat[...] = gfeat_in[...]
    gself[...] = wall[pl.ds(0, half)].reshape(gself.shape).astype(F32)
    gneigh[...] = wall[pl.ds(half, half)].reshape(gneigh.shape).astype(F32)


def body(
    nrow, nrep,
    features, weight_self, weight_neigh, degrees, tile_values, tile_blocks, tile_count, cotangent,
):
    rows, width = features.shape
    here, slots, tile = tile_values.shape[1], tile_values.shape[2], tile_values.shape[-1]
    share = rows // nrep
    half = nrow // PAIR
    ny = half // PAIR
    piece = 2 * width // nrow
    lanes = 128
    slices = width // lanes
    assert here == PAIR and half == nrep and (rows // tile) ** 2 <= 128 and slots <= 128
    sems = pltpu.SemaphoreType.DMA
    vmem = pl.BlockSpec(memory_space=pltpu.VMEM)
    anywhere = pl.BlockSpec(memory_space=pl.ANY)

    def buf(*shape):
        return pltpu.VMEM(shape, BF16)

    out, wall, gfeat = pl.pallas_call(
        functools.partial(layer_kernel, nrow, nrep, here),
        out_shape=(
            jax.ShapeDtypeStruct((share, width), BF16),
            jax.ShapeDtypeStruct((nrow, piece, width), BF16),
            jax.ShapeDtypeStruct((share, width), BF16),
        ),
        in_specs=[anywhere] + [vmem] * 4 + [anywhere, vmem, pl.BlockSpec(memory_space=pltpu.SMEM)],
        out_specs=(vmem,) * 3,
        scratch_shapes=[
            buf(here, slots, tile, tile),
            pltpu.VMEM((slots + 1, tile, tile), F32),
            buf(here, rows, rows),
            pltpu.VMEM((8, 128), jnp.int32),
            pltpu.VMEM((8, 128), jnp.int32),
            pltpu.SMEM((8, 128), jnp.int32),
            buf(share, width),
            buf(slices, nrow, share, lanes),
            pltpu.VMEM((slices, share, lanes), F32),
            buf(slices, nrep - 1, share, lanes),
            buf(slices, nrep - 1, share, lanes),
            buf(share, width),
            buf(share, width),
            buf(slices, nrep, share, lanes),
            buf(lanes, rows),
            buf(slices, nrow, lanes, share),
            buf(slices, nrep, lanes, share),
            buf(slices, half - 1, lanes, share),
            buf(slices, half - 1, lanes, share),
            buf(slices, lanes, share),
            buf(slices, lanes, share),
            buf(nrow, piece, width),
            buf(nrow - 1, piece, width),
            buf(nrep, piece, width),
            pltpu.VMEM((share, width), F32),
            pltpu.VMEM((rows, tile), F32),
            sems((here,)), sems, sems, sems((slices, nrep)),
            sems((slices, nrep, ny)), sems((slices, nrep)), sems((slices, nrep)), sems((slices, nrep)),
            sems((slices, nrep - 1)), sems((slices, nrep - 1)),
            sems((nrep - 1, PARTS)), sems((nrep - 1, PARTS)),
            sems((slices, nrep - 1, PARTS)), sems((slices, nrep - 1, PARTS)),
            sems, sems,
            sems((nrow - 1,)), sems((nrow - 1,)),
            sems((nrep - 1,)), sems((nrep - 1,)),
            sems((nrow - 1,)), sems((nrow - 1,)),
            sems((slices, nrep)), sems((slices, nrep)),
            sems((slices, half - 1)), sems((slices, half - 1)),
            sems((slices,)), sems((slices,)),
        ],
        compiler_params=pltpu.CompilerParams(collective_id=0, has_side_effects=True),
        name="layer",
    )(
        features, weight_self, weight_neigh, degrees.reshape(rows // tile, tile), cotangent,
        tile_values[0], tile_blocks.transpose(0, 1, 3, 2)[0], tile_count[0],
    )
    out, grad_self, grad_neigh, gfeat = pl.pallas_call(
        close_kernel,
        out_shape=(
            jax.ShapeDtypeStruct((share, width), BF16),
            jax.ShapeDtypeStruct((width, width), F32),
            jax.ShapeDtypeStruct((width, width), F32),
            jax.ShapeDtypeStruct((share, width), BF16),
        ),
        in_specs=[vmem] * 3,
        out_specs=(vmem,) * 4,
        name="close",
    )(out, wall, gfeat)
    return out, grad_self, grad_neigh, gfeat


def solution(mesh):
    in_specs = (
        P("row", None),
        P(),
        P(),
        P("row"),
        P("row", "rep", None, None, None),
        P("row", "rep", None, None),
        P("row", "rep"),
        P(("row", "rep"), None),
    )
    out_specs = (P(("row", "rep"), None), P(), P(), P(("row", "rep"), None))
    run = functools.partial(body, mesh.shape["row"], mesh.shape["rep"])
    return jax.shard_map(run, mesh=mesh, in_specs=in_specs, out_specs=out_specs, check_vma=False)
```

```python
import functools

import jax
import jax.numpy as jnp
from jax import lax
from jax.experimental import pallas as pl
from jax.experimental.pallas import tpu as pltpu
from jax.sharding import PartitionSpec as P

MESH = pl.DeviceIdType.MESH
F32 = jnp.float32
BF16 = jnp.bfloat16
PAIR = 2
PARTS = 4
SPLIT = 2
STRAIGHT = 1
NOW = 0
MAJOR = 1
TAIL = (2, 2)
DIRECT = (1,)
ORDER = 1
KSPLIT = 1
STOP = 99


def remote(src, dst, send, recv, device):
    return pltpu.make_async_remote_copy(
        src_ref=src, dst_ref=dst, send_sem=send, recv_sem=recv, device_id=device, device_id_type=MESH
    )


def cut(width, shares):
    spans, at = [], 0
    for s in shares:
        spans.append((at, width // s))
        at += width // s
    assert at == width
    return spans


def bits_of(n):
    return (n - 1).bit_length()


def xor(a, b, n):
    total = 0
    for k in range(bits_of(n)):
        w = 2**k
        total = total + ((a // w + b // w) % 2) * w
    return total


def mirror(a, n):
    total = 0
    top = bits_of(n)
    for k in range(top):
        total = total + ((a // 2**k) % 2) * 2 ** (top - 1 - k)
    return total


def layer_kernel(
    nrow, nrep, here,
    feat_hbm, wself_hbm, wneigh_hbm, deg_hbm, cot_hbm, tiles_hbm, blocks_hbm, count_hbm,
    out, wall, gfeat,
    wself, wneigh, deg, cot, blocks, count, tiles, runs, adj, keys, tab_v, tab_s, my_feat, src, mine, part, part_in, agg_all, gpre_all,
    dagg, late, acc, late_acc, terms, pair_in, summed, plane_in, back, back_in, straight, straight_in,
    wpart, wrow_in, wrep_in, base, deg_col,
    small_sem, tile_sem, tab_sem, feat_sem, own_sem,
    p1s, p1r, p1ps, p1pr, bs, br, es, er, cs, cr, w1s, w1r, w2s, w2r, w3s, w3r, w3ps, w3pr,
    d0s, d0r, d1s, d1r, d2s, d2r, d3s, d3r, ts, tr, t0s, t0r, t1s, t1r, t2s, t2r,
):
    row, rep = lax.axis_index("row"), lax.axis_index("rep")
    rows, width = feat_hbm.shape
    lanes = src.shape[-1]
    slices = width // lanes
    share = rows // nrep
    half = nrow // PAIR
    tile = tiles.shape[-1]
    slots = tiles.shape[1]
    nblk = rows // tile
    hi, lo = row // PAIR, row % PAIR
    hx, hy = hi % PAIR, hi // PAIR
    ny = half // PAIR
    sx, sy = rep % PAIR, rep // PAIR
    is_src = hi == rep
    is_x = jnp.logical_and(hy == sy, hx != sx)
    is_y = jnp.logical_and(hx == sx, hy != sy)
    is_d = jnp.logical_and(hx != sx, hy != sy)
    partner = (hi * PAIR + (1 - lo), rep)
    my_q = xor(hi, mirror(rep, nrep), nrep)
    owner = (rep * PAIR + lo, my_q)
    moves = jnp.logical_or(owner[0] != row, owner[1] != rep)
    pieces = nrep * SPLIT
    grain = rows // pieces

    def ordered(i):
        place = 0
        for r in range(nrep):
            by_distance = sorted((k for k in range(nrep) if k != r), key=lambda k: (-abs(k - r), k))
            place = place + jnp.where(rep == r, by_distance[i], 0)
        return place

    far = [ordered(i) for i in range(nrep - 1)]

    barrier = pltpu.get_barrier_semaphore()

    def greet(device):
        pl.semaphore_signal(barrier, inc=1, device_id=device, device_id_type=MESH)

    for d in range(1, nrow):
        greet(((row + d) % nrow, rep))
    for d in range(1, nrep):
        greet((row, (rep + d) % nrep))

    for k in range(nrep):
        @pl.when(jnp.logical_or(hi != rep, rep != k))
        def _():
            greet((rep * PAIR + lo, k))
            greet((k * PAIR + lo, hi))

    def own_copy(c, k):
        return pltpu.make_async_copy(
            feat_hbm.at[pl.ds(k * grain, grain), pl.ds(c * lanes, lanes)],
            src.at[c, lo * pieces + k], own_sem.at[c, k],
        )

    @pl.when(is_src)
    def _():
        for c in range(slices):
            for k in range(pieces):
                own_copy(c, k).start()

    small = [
        pltpu.make_async_copy(a, b, small_sem.at[i])
        for i, (a, b) in enumerate((
            (blocks_hbm, blocks), (count_hbm, count), (deg_hbm, deg),
            (wself_hbm, wself), (wneigh_hbm, wneigh), (cot_hbm, cot),
        ))
    ]
    for copy in small:
        copy.start()
    tile_copies = [
        pltpu.make_async_copy(tiles_hbm.at[j], tiles.at[j], tile_sem.at[j]) for j in range(here)
    ]
    for copy in tile_copies:
        copy.start()
    feat_copy = pltpu.make_async_copy(
        feat_hbm.at[pl.ds(pl.multiple_of(rep * share, share), share)], my_feat, feat_sem
    )
    feat_copy.start()

    pl.semaphore_wait(barrier, nrow - 1 + nrep - 1 + 2 * (nrep - is_src.astype(jnp.int32)))

    def hop(c, k, i, h):
        at = src.at[c, lo * pieces + k]
        return remote(at, at, p1s.at[c, k, i], p1r.at[c, k], (h * PAIR + lo, rep))

    def x_peer():
        return hy * PAIR + (1 - hx)

    def y_peer(d):
        return ((hy + d) % ny) * PAIR + hx

    def to_partner(c, k):
        at = src.at[c, lo * pieces + k]
        return remote(at, at, p1ps.at[c, k], p1pr.at[c, k], partner)

    def from_partner(c, k):
        at = src.at[c, (1 - lo) * pieces + k]
        return remote(at, at, p1ps.at[c, k], p1pr.at[c, k], partner)

    first, second = list(range(pieces // 2)), list(range(pieces // 2, pieces))

    @pl.when(is_src)
    def _():
        for c in range(slices):
            for k in range(pieces):
                own_copy(c, k).wait()
            for kx, ky in zip(first + second, second + first):
                hop(c, kx, 0, x_peer()).start()
                for d in range(1, ny):
                    hop(c, ky, d, y_peer(d)).start()
            for k in range(pieces):
                to_partner(c, k).start()

    for copy in small:
        copy.wait()
    side = keys.shape[-1]
    at_row = lax.broadcasted_iota(jnp.int32, (side, side), 0)
    at_col = lax.broadcasted_iota(jnp.int32, (side, side), 1)
    for j in range(here):
        keys[...] = jnp.full(keys.shape, -1, jnp.int32)
        keys[0:1, 0:slots] = blocks[j, 0:1, :] * nblk + blocks[j, 1:2, :]
        line = jnp.broadcast_to(keys[0:1, :], (side, side))
        column = line.T
        before = jnp.where(jnp.logical_and(column == line, at_row < at_col), at_row + 1, 0)
        latest = jnp.where(jnp.logical_and(column == at_col, at_row < count[j]), at_row + 1, 0)
        tab_v[2 * j : 2 * j + 1, :] = jnp.max(before, axis=0, keepdims=True)
        tab_v[2 * j + 1 : 2 * j + 2, :] = jnp.max(latest, axis=0, keepdims=True)
    tab_copy = pltpu.make_async_copy(tab_v, tab_s, tab_sem)
    tab_copy.start()
    run = deg.shape[1]
    for b in range(rows // run):
        line = jnp.broadcast_to(deg[b : b + 1, :].astype(F32), (run, run))
        deg_col[pl.ds(b * run, run), :] = line.T
    tab_copy.wait()

    for j in range(here):
        tile_copies[j].wait()
        runs[0] = jnp.zeros((tile, tile), F32)

        def add(slot, carry):
            runs[slot + 1] = tiles[j, slot].astype(F32) + runs[tab_s[2 * j, slot]]
            return carry

        lax.fori_loop(0, slots, add, 0)

        def place(b, carry):
            for c in range(nblk):
                block = runs[tab_s[2 * j + 1, b * nblk + c]]
                adj[j, pl.ds(pl.multiple_of(b * tile, tile), tile), c * tile : (c + 1) * tile] = block.astype(BF16)
            return carry

        lax.fori_loop(0, nblk, place, 0)

    def relay(c):
        @pl.when(is_x)
        def _():
            for k in first + second:
                hop(c, k, 0, hi).wait_recv()
                if k in first:
                    for d in range(1, ny):
                        hop(c, k, d, y_peer(d)).start()
                to_partner(c, k).start()

        @pl.when(is_y)
        def _():
            for k in second + first:
                hop(c, k, 0, hi).wait_recv()
                if k in second:
                    hop(c, k, 0, x_peer()).start()
                to_partner(c, k).start()

        @pl.when(is_d)
        def _():
            for pair in zip(first, second):
                for k in pair:
                    hop(c, k, 0, hi).wait_recv()
                    to_partner(c, k).start()

        for k in range(pieces):
            from_partner(c, k).wait_recv()

    def partial(c, at, n):
        total = jnp.zeros((n, lanes), F32)
        for j in range(here):
            a = adj[j, pl.ds(pl.multiple_of(at, n), n), :]
            f = src[c, pl.ds(j * pieces, pieces)].reshape(rows, lanes)
            total = total + jnp.dot(a, f, preferred_element_type=F32)
        return total

    last = slices - 1
    step = share // PARTS

    def send_dagg(c, to, i):
        at = dagg.at[c, rep, pl.ds(i * step, step)]
        return remote(at, at, cs.at[c, to, i], cr.at[c, rep, i], (row, to))

    tail = cut(lanes, TAIL)

    def send_late(n, to):
        f0, fs = tail[n]
        at = late.at[rep, pl.ds(f0, fs)]
        return remote(at, at, ts.at[n, to], tr.at[n, rep], (row, to))

    def get_late(n, k):
        f0, fs = tail[n]
        at = late.at[k, pl.ds(f0, fs)]
        return remote(at, at, ts.at[n, k], tr.at[n, k], (row, k))

    def get_dagg(c, k, i):
        at = dagg.at[c, k, pl.ds(i * step, step)]
        return remote(at, at, cs.at[c, k, i], cr.at[c, k, i], (row, k))

    def send_part(c, to):
        return remote(
            part.at[c, to], part_in.at[c, rep], bs.at[c, to], br.at[c, rep], (row, to)
        )

    def get_part(c, k):
        return remote(part_in.at[c, k], part_in.at[c, k], bs.at[c, k], br.at[c, k], (row, k))

    def send_step(to, i):
        steps = pl.ds(i * step, step)
        return remote(
            part.at[last, to, steps], part_in.at[last, rep, steps], es.at[to, i], er.at[rep, i], (row, to)
        )

    def get_step(k, i):
        at = part_in.at[last, k, pl.ds(i * step, step)]
        return remote(at, at, es.at[k, i], er.at[k, i], (row, k))

    def finish(level):
        @pl.when(is_src)
        def _():
            for c in range(slices):
                for k in range(pieces):
                    hop(c, k, 0, x_peer()).wait_send()
                    for d in range(1, ny):
                        hop(c, k, d, y_peer(d)).wait_send()

        @pl.when(is_x)
        def _():
            for c in range(slices):
                for k in first:
                    for d in range(1, ny):
                        hop(c, k, d, y_peer(d)).wait_send()

        @pl.when(is_y)
        def _():
            for c in range(slices):
                for k in second:
                    hop(c, k, 0, x_peer()).wait_send()

        for c in range(slices):
            for k in range(pieces):
                to_partner(c, k).wait_send()
            for to in far:
                if level >= 2:
                    if c < last:
                        send_part(c, to).wait_send()
                    else:
                        for i in range(PARTS):
                            send_step(to, i).wait_send()
                if level >= 3 and c < last:
                    for i in range(PARTS):
                        send_dagg(c, to, i).wait_send()
            if level >= 4 and c < last:
                for q in range(nrep):
                    send_pair(c, q).wait_send()
            if level >= 9 and c < last:
                for e in range(1, half):
                    send_plane(c, e).wait_send()

                @pl.when(moves)
                def _():
                    to_owner(c).wait_send()
        if level >= 3:
            for d in range(1, nrow):
                send_w1(d).wait_send()
        if level >= 9:
            for n in range(len(tail)):
                for q in range(nrep):
                    send_late_pair(n, q).wait_send()
                for to in far:
                    send_late(n, to).wait_send()
                    if n in DIRECT:
                        straight_to(n, to).wait_send()
                if n not in DIRECT:
                    for e in range(1, half):
                        send_late_plane(n, e).wait_send()

                    @pl.when(moves)
                    def _():
                        late_to_owner(n).wait_send()

            @pl.when(jnp.logical_not(is_src))
            def _():
                for n in DIRECT:
                    straight_to(n, rep).wait_send()

        if level >= 9:
            for d in range(1, nrep if not NOW else 1):
                send_w2(d).wait_send()
            for e in range(half if not NOW else 0):
                if e > 0:
                    send_w3(e).wait_send()
                share_w3(e).wait_send()

    for c in range(slices):
        relay(c)
        if STOP == 1:
            continue
        if c < last:
            for to in far:
                part[c, to] = partial(c, to * share, share).astype(BF16)
                send_part(c, to).start()
        elif MAJOR:
            for i in range(PARTS):
                for to in far:
                    part[c, to, pl.ds(i * step, step)] = partial(c, to * share + i * step, step).astype(BF16)
                    send_step(to, i).start()
        else:
            for to in far:
                part[c, to] = partial(c, to * share, share).astype(BF16)
            for i in range(PARTS):
                for to in far:
                    send_step(to, i).start()
        mine[c] = partial(c, rep * share, share)
    feat_copy.wait()
    if STOP == 1:
        finish(1)
        return
    base[...] = jnp.dot(my_feat[...], wself[...], preferred_element_type=F32)

    for c in range(last):
        for k in far:
            get_part(c, k).wait_recv()
            mine[c] = mine[c] + part_in[c, k].astype(F32)
    for i in range(PARTS):
        at = pl.ds(i * step, step)
        degree = deg_col[pl.ds(pl.multiple_of(rep * share + i * step, step), step), :]
        total = mine[last, at]
        for k in far:
            get_step(k, i).wait_recv()
            total = total + part_in[last, k, at].astype(F32)
        sums = [mine[c, at] for c in range(last)] + [total]
        agg = jnp.concatenate([(s / degree).astype(BF16) for s in sums], axis=1)
        agg_all[at] = agg
        pre = base[at] + jnp.dot(agg, wneigh[...], preferred_element_type=F32)
        sig = jax.nn.sigmoid(pre)
        gpre = (cot[at].astype(F32) * sig * (1.0 + pre * (1.0 - sig))).astype(BF16)
        gpre_all[at] = gpre
        back_t = lax.dot_general(gpre, wneigh[...], (((1,), (1,)), ((), ())), preferred_element_type=F32)
        for c in range(slices):
            dagg[c, rep, at] = (back_t[:, c * lanes : (c + 1) * lanes] / degree).astype(BF16)
        if STOP > 2:
            for to in far:
                send_dagg(0, to, i).start()
        out[at] = (pre * sig).astype(BF16)
    if STOP == 2:
        finish(2)
        return
    late[rep] = dagg[last, rep].T
    for n in range(len(tail)):
        for to in far:
            send_late(n, to).start()

    gpre = gpre_all[...]
    ws = lax.dot_general(my_feat[...], gpre, (((0,), (0,)), ((), ())), preferred_element_type=F32)
    wn = lax.dot_general(agg_all[...], gpre, (((0,), (0,)), ((), ())), preferred_element_type=F32)
    piece = wpart.shape[1]
    wpart[pl.ds(0, half)] = ws.astype(BF16).reshape(half, piece, width)
    wpart[pl.ds(half, half)] = wn.astype(BF16).reshape(half, piece, width)

    def send_w1(d):
        to = (row + d) % nrow
        return remote(wpart.at[to], wrow_in.at[d - 1], w1s.at[d - 1], w1r.at[d - 1], (to, rep))

    for d in range(1, nrow):
        send_w1(d).start()
    base[...] = lax.dot_general(gpre, wself[...], (((1,), (1,)), ((), ())), preferred_element_type=F32)

    unit = max(share, 128)
    per_unit = unit // share

    def send_pair(c, q):
        return remote(
            terms.at[c, (1 - lo) * nrep + q], pair_in.at[c, q], d0s.at[c, q], d0r.at[c, q], partner
        )

    def send_plane(c, e):
        return remote(
            summed.at[c, e - 1], plane_in.at[c, e - 1], d1s.at[c, e - 1], d1r.at[c, e - 1],
            (xor(hi, e, half) * PAIR + lo, rep),
        )

    def to_owner(c):
        return remote(back.at[c], back_in.at[c], d2s.at[c], d2r.at[c], owner)

    def straight_to(n, q):
        f0, fs = tail[n]
        return remote(
            straight.at[q, pl.ds(f0, fs)], straight_in.at[hi, pl.ds(f0, fs)],
            d3s.at[n, q], d3r.at[n, hi], (rep * PAIR + lo, q),
        )

    def straight_from(n, k):
        f0, fs = tail[n]
        at = straight_in.at[k, pl.ds(f0, fs)]
        return remote(at, at, d3s.at[n, k], d3r.at[n, k], (k * PAIR + lo, hi))

    def send_late_pair(n, q):
        f0, fs = tail[n]
        return remote(
            terms.at[last, (1 - lo) * nrep + q, pl.ds(f0, fs)], pair_in.at[last, q, pl.ds(f0, fs)],
            t0s.at[n, q], t0r.at[n, q], partner,
        )

    def gain(sums, f0, fs, left, k, start, emit):
        for j in (1 - lo, lo):
            slot = 0 if j is lo else 1
            for u in range(rows // unit):
                a = adj[j, pl.ds(pl.multiple_of(k * share, share), share), u * unit : (u + 1) * unit]
                t = jnp.dot(left, a, preferred_element_type=F32)
                if not start:
                    t = t + sums[slot, u, f0 : f0 + fs, :]
                if emit is None:
                    sums[slot, u, f0 : f0 + fs, :] = t
                    continue
                t = t.astype(BF16)
                for v in range(per_unit):
                    emit(j, u * per_unit + v, t[:, v * share : (v + 1) * share])

    def emit_early(j, q, value):
        terms[0, j * nrep + q] = value
        if j is not lo:
            send_pair(0, q).start()

    def emit_late(n):
        f0, fs = tail[n]

        def emit(j, q, value):
            terms[last, j * nrep + q, f0 : f0 + fs, :] = value
            if j is not lo:
                send_late_pair(n, q).start()

        return emit

    def make_own():
        gain(acc, 0, lanes, dagg[0, rep].T, rep, True, None)
        gain(late_acc, 0, lanes, late[rep], rep, True, None)

    def make_early():
        near = far[::-1]
        for k in near:
            for i in range(PARTS):
                get_dagg(0, k, i).wait_recv()
            gain(acc, 0, lanes, dagg[0, k].T, k, False, emit_early if k is near[-1] else None)

    def make_late(n):
        f0, fs = tail[n]
        near = far[::-1]
        for k in near:
            get_late(n, k).wait_recv()
            gain(late_acc, f0, fs, late[k, f0 : f0 + fs, :], k, False, emit_late(n) if k is near[-1] else None)

    def send_late_plane(n, e):
        f0, fs = tail[n]
        at = (last, e - 1, pl.ds(f0, fs))
        return remote(
            summed.at[at], plane_in.at[at], t1s.at[n, e - 1], t1r.at[n, e - 1],
            (xor(hi, e, half) * PAIR + lo, rep),
        )

    def late_to_owner(n):
        f0, fs = tail[n]
        at = (last, pl.ds(f0, fs))
        return remote(back.at[at], back_in.at[at], t2s.at[n], t2r.at[n], owner)

    def add_late_plane(n):
        f0, fs = tail[n]
        both = back_sum[n + 1]
        for e in range(1, half):
            send_late_plane(n, e).wait_recv()
            both = both + plane_in[last, e - 1, f0 : f0 + fs, :].astype(F32)
        back[last, f0 : f0 + fs, :] = both.astype(BF16)

        @pl.when(moves)
        def _():
            late_to_owner(n).start()

    def add_late_pair(n):
        f0, fs = tail[n]
        if n not in DIRECT:
            for e in list(range(half - 1, 0, -1)) + [0]:
                q = xor(xor(hi, e, half), mirror(rep, nrep), nrep)
                send_late_pair(n, q).wait_recv()
                both = terms[last, lo * nrep + q, f0 : f0 + fs, :].astype(F32)
                both = both + pair_in[last, q, f0 : f0 + fs, :].astype(F32)
                if e > 0:
                    summed[last, e - 1, f0 : f0 + fs, :] = both.astype(BF16)
                    send_late_plane(n, e).start()
                else:
                    back_sum[n + 1] = both
            return
        for q in far + [rep]:
            send_late_pair(n, q).wait_recv()
            both = terms[last, lo * nrep + q, f0 : f0 + fs, :].astype(F32)
            both = (both + pair_in[last, q, f0 : f0 + fs, :].astype(F32)).astype(BF16)
            straight[q, f0 : f0 + fs, :] = both
            if q is rep:
                @pl.when(jnp.logical_not(is_src))
                def _():
                    straight_to(n, q).start()

                @pl.when(is_src)
                def _():
                    straight_in[hi, f0 : f0 + fs, :] = both
            else:
                straight_to(n, q).start()

    def add_pair(c):
        for e in list(range(half - 1, 0, -1)) + [0]:
            q = xor(xor(hi, e, half), mirror(rep, nrep), nrep)
            send_pair(c, q).wait_recv()
            both = terms[c, lo * nrep + q].astype(F32) + pair_in[c, q].astype(F32)
            if e > 0:
                summed[c, e - 1] = both.astype(BF16)
                send_plane(c, e).start()
            else:
                back_sum[c] = both

    def add_plane(c):
        both = back_sum[c]
        for e in range(1, half):
            send_plane(c, e).wait_recv()
            both = both + plane_in[c, e - 1].astype(F32)
        back[c] = both.astype(BF16)

        @pl.when(moves)
        def _():
            to_owner(c).start()

    back_sum = {}
    if NOW:
        for d in range(1, nrow):
            send_w1(d).wait_recv()
    def send_w2(d):
        return remote(
            wrep_in.at[rep], wrep_in.at[rep], w2s.at[d - 1], w2r.at[d - 1], (row, (rep + d) % nrep)
        )

    def send_w3(e):
        return remote(
            wall.at[row], wall.at[row], w3s.at[e - 1], w3r.at[e - 1], (xor(hi, e, half) * PAIR + lo, rep)
        )

    def get_w3(e):
        at = wall.at[xor(hi, e, half) * PAIR + lo]
        return remote(at, at, w3s.at[e - 1], w3r.at[e - 1], (row, rep))

    def share_w3(e):
        at = wall.at[xor(hi, e, half) * PAIR + lo]
        return remote(at, at, w3ps.at[e], w3pr.at[e], partner)

    def shared_w3(e):
        at = wall.at[xor(hi, e, half) * PAIR + (1 - lo)]
        return remote(at, at, w3ps.at[e], w3pr.at[e], partner)

    def reduce_rows():
        wsum = wpart[row].astype(F32)
        for d in range(1, nrow):
            send_w1(d).wait_recv()
            wsum = wsum + wrow_in[d - 1].astype(F32)
        wrep_in[rep] = wsum.astype(BF16)
        for d in range(1, nrep):
            send_w2(d).start()

    def reduce_reps():
        for d in range(1, nrep):
            remote(
                wrep_in.at[rep], wrep_in.at[(rep + nrep - d) % nrep], w2s.at[d - 1], w2r.at[d - 1], (row, rep)
            ).wait_recv()
        wsum = wrep_in[0].astype(F32)
        for k in range(1, nrep):
            wsum = wsum + wrep_in[k].astype(F32)
        wall[row] = wsum.astype(BF16)
        for e in range(1, half):
            send_w3(e).start()
        share_w3(0).start()

    make_own()
    make_early()
    add_pair(0)
    if not NOW:
        reduce_rows()
    for n in range(len(tail)):
        make_late(n)
        add_late_pair(n)
    for c in range(last):
        add_plane(c)
    if ORDER == 1 and not NOW:
        reduce_reps()
    for n in range(len(tail)):
        if n not in DIRECT:
            add_late_plane(n)
    if ORDER == 2 and not NOW:
        reduce_reps()
    if not NOW:
        for e in range(1, half):
            get_w3(e).wait_recv()
            share_w3(e).start()

    for c in range(last):
        cols = slice(c * lanes, (c + 1) * lanes)

        @pl.when(moves)
        def _():
            to_owner(c).wait_recv()
            gfeat[:, cols] = (base[:, cols] + back_in[c].astype(F32).T).astype(BF16)

        @pl.when(jnp.logical_not(moves))
        def _():
            gfeat[:, cols] = (base[:, cols] + back[c].astype(F32).T).astype(BF16)

    for n, (f0, fs) in enumerate(tail):
        if n not in DIRECT:
            cols = slice(last * lanes + f0, last * lanes + f0 + fs)

            @pl.when(moves)
            def _():
                late_to_owner(n).wait_recv()
                gfeat[:, cols] = (base[:, cols] + back_in[last, f0 : f0 + fs, :].astype(F32).T).astype(BF16)

            @pl.when(jnp.logical_not(moves))
            def _():
                gfeat[:, cols] = (base[:, cols] + back[last, f0 : f0 + fs, :].astype(F32).T).astype(BF16)

            continue
        for k in range(half):
            @pl.when(jnp.logical_or(rep != hi, hi != k))
            def _():
                straight_from(n, k).wait_recv()

        both = jnp.zeros((fs, share), F32)
        for k in range(half):
            both = both + straight_in[k, f0 : f0 + fs, :].astype(F32)
        both = both.astype(BF16).astype(F32)
        at = last * lanes + f0
        gfeat[:, at : at + fs] = (base[:, at : at + fs] + both.T).astype(BF16)
    if not NOW:
        for e in range(half):
            shared_w3(e).wait_recv()
    finish(9)


def close_kernel(out_in, wall, gfeat_in, out, gself, gneigh, gfeat):
    half = wall.shape[0] // 2
    out[...] = out_in[...]
    gfeat[...] = gfeat_in[...]
    gself[...] = wall[pl.ds(0, half)].reshape(gself.shape).astype(F32)
    gneigh[...] = wall[pl.ds(half, half)].reshape(gneigh.shape).astype(F32)


def body(
    nrow, nrep,
    features, weight_self, weight_neigh, degrees, tile_values, tile_blocks, tile_count, cotangent,
):
    rows, width = features.shape
    here, slots, tile = tile_values.shape[1], tile_values.shape[2], tile_values.shape[-1]
    share = rows // nrep
    half = nrow // PAIR
    ny = half // PAIR
    piece = 2 * width // nrow
    lanes = 128
    slices = width // lanes
    pieces = nrep * SPLIT
    unit = max(share, 128)
    nt = len(TAIL)
    assert slices == 2 and here == PAIR and half == nrep and (rows // tile) ** 2 <= 128 and slots <= 128
    sems = pltpu.SemaphoreType.DMA
    vmem = pl.BlockSpec(memory_space=pltpu.VMEM)
    anywhere = pl.BlockSpec(memory_space=pl.ANY)

    def buf(*shape):
        return pltpu.VMEM(shape, BF16)

    out, wall, gfeat = pl.pallas_call(
        functools.partial(layer_kernel, nrow, nrep, here),
        out_shape=(
            jax.ShapeDtypeStruct((share, width), BF16),
            jax.ShapeDtypeStruct((nrow, piece, width), BF16),
            jax.ShapeDtypeStruct((share, width), BF16),
        ),
        in_specs=[anywhere] * 8,
        out_specs=(vmem,) * 3,
        scratch_shapes=[
            buf(width, width), buf(width, width),
            pltpu.VMEM((rows // tile, tile), jnp.int32),
            buf(share, width),
            pltpu.VMEM((here, 2, slots), jnp.int32),
            pltpu.SMEM((here,), jnp.int32),
            buf(here, slots, tile, tile),
            pltpu.VMEM((slots + 1, tile, tile), F32),
            buf(here, rows, rows),
            pltpu.VMEM((8, 128), jnp.int32),
            pltpu.VMEM((8, 128), jnp.int32),
            pltpu.SMEM((8, 128), jnp.int32),
            buf(share, width),
            buf(slices, here * pieces, rows // pieces, lanes),
            pltpu.VMEM((slices, share, lanes), F32),
            buf(slices, nrep, share, lanes),
            buf(slices, nrep, share, lanes),
            buf(share, width),
            buf(share, width),
            buf(slices, nrep, share, lanes),
            buf(nrep, lanes, share),
            pltpu.VMEM((here, rows // unit, lanes, unit), F32),
            pltpu.VMEM((here, rows // unit, lanes, unit), F32),
            buf(slices, nrow, lanes, share),
            buf(slices, nrep, lanes, share),
            buf(slices, half - 1, lanes, share),
            buf(slices, half - 1, lanes, share),
            buf(slices, lanes, share),
            buf(slices, lanes, share),
            buf(nrep, lanes, share),
            buf(half, lanes, share),
            buf(nrow, piece, width),
            buf(nrow - 1, piece, width),
            buf(nrep, piece, width),
            pltpu.VMEM((share, width), F32),
            pltpu.VMEM((rows, tile), F32),
            sems((6,)), sems((here,)), sems, sems, sems((slices, pieces)),
            sems((slices, pieces, ny)), sems((slices, pieces)), sems((slices, pieces)), sems((slices, pieces)),
            sems((slices, nrep)), sems((slices, nrep)),
            sems((nrep, PARTS)), sems((nrep, PARTS)),
            sems((slices, nrep, PARTS)), sems((slices, nrep, PARTS)),
            sems((nrow - 1,)), sems((nrow - 1,)),
            sems((nrep - 1,)), sems((nrep - 1,)),
            sems((half - 1,)), sems((half - 1,)), sems((half,)), sems((half,)),
            sems((slices, nrep)), sems((slices, nrep)),
            sems((slices, half - 1)), sems((slices, half - 1)),
            sems((slices,)), sems((slices,)),
            sems((nt, nrep)), sems((nt, half)), sems((nt, nrep)), sems((nt, nrep)),
            sems((nt, nrep)), sems((nt, nrep)),
            sems((nt, half - 1)), sems((nt, half - 1)), sems((nt,)), sems((nt,)),
        ],
        compiler_params=pltpu.CompilerParams(collective_id=0, has_side_effects=True),
        name="layer",
    )(
        features, weight_self, weight_neigh, degrees.reshape(rows // tile, tile), cotangent,
        tile_values[0], tile_blocks.transpose(0, 1, 3, 2)[0], tile_count[0],
    )
    out, grad_self, grad_neigh, gfeat = pl.pallas_call(
        close_kernel,
        out_shape=(
            jax.ShapeDtypeStruct((share, width), BF16),
            jax.ShapeDtypeStruct((width, width), F32),
            jax.ShapeDtypeStruct((width, width), F32),
            jax.ShapeDtypeStruct((share, width), BF16),
        ),
        in_specs=[vmem] * 3,
        out_specs=(vmem,) * 4,
        name="close",
    )(out, wall, gfeat)
    return out, grad_self, grad_neigh, gfeat


def solution(mesh):
    in_specs = (
        P("row", None),
        P(),
        P(),
        P("row"),
        P("row", "rep", None, None, None),
        P("row", "rep", None, None),
        P("row", "rep"),
        P(("row", "rep"), None),
    )
    out_specs = (P(("row", "rep"), None), P(), P(), P(("row", "rep"), None))
    run = functools.partial(body, mesh.shape["row"], mesh.shape["rep"])
    return jax.shard_map(run, mesh=mesh, in_specs=in_specs, out_specs=out_specs, check_vma=False)
```

```python
import functools

import jax
import jax.numpy as jnp
from jax import lax
from jax.experimental import pallas as pl
from jax.experimental.pallas import tpu as pltpu
from jax.sharding import PartitionSpec as P

MESH = pl.DeviceIdType.MESH
F32 = jnp.float32
BF16 = jnp.bfloat16
PAIR = 2
PARTS = 4
SPLIT = 2
TAIL = (5, 3)
DIRECT = (1,)


def remote(src, dst, send, recv, device):
    return pltpu.make_async_remote_copy(
        src_ref=src, dst_ref=dst, send_sem=send, recv_sem=recv, device_id=device, device_id_type=MESH
    )


def cut(width, shares):
    spans, at = [], 0
    for s in shares:
        spans.append((at, width * s // sum(shares)))
        at += width * s // sum(shares)
    assert at == width
    return spans


def bits_of(n):
    return (n - 1).bit_length()


def xor(a, b, n):
    total = 0
    for k in range(bits_of(n)):
        w = 2**k
        total = total + ((a // w + b // w) % 2) * w
    return total


def mirror(a, n):
    total = 0
    top = bits_of(n)
    for k in range(top):
        total = total + ((a // 2**k) % 2) * 2 ** (top - 1 - k)
    return total


def layer_kernel(
    nrow, nrep, here,
    feat_hbm, wself_hbm, wneigh_hbm, deg_hbm, cot_hbm, tiles_hbm, blocks_hbm, count_hbm,
    out, wall, gfeat,
    wself, wneigh, deg, cot, blocks, count, tiles, runs, adj, keys, tab_v, tab_s, my_feat, src, mine, part, part_in, agg_all, gpre_all,
    dagg, late, acc, late_acc, terms, pair_in, summed, plane_in, back, back_in, straight, straight_in,
    wpart, wrow_in, wrep_in, base, deg_col,
    small_sem, tile_sem, tab_sem, feat_sem, own_sem,
    p1s, p1r, p1ps, p1pr, bs, br, es, er, cs, cr, w1s, w1r, w2s, w2r, w3s, w3r, w3ps, w3pr,
    d0s, d0r, d1s, d1r, d2s, d2r, d3s, d3r, ts, tr, t0s, t0r, t1s, t1r, t2s, t2r,
):
    row, rep = lax.axis_index("row"), lax.axis_index("rep")
    rows, width = feat_hbm.shape
    lanes = src.shape[-1]
    slices = width // lanes
    share = rows // nrep
    half = nrow // PAIR
    tile = tiles.shape[-1]
    slots = tiles.shape[1]
    nblk = rows // tile
    hi, lo = row // PAIR, row % PAIR
    hx, hy = hi % PAIR, hi // PAIR
    ny = half // PAIR
    sx, sy = rep % PAIR, rep // PAIR
    is_src = hi == rep
    is_x = jnp.logical_and(hy == sy, hx != sx)
    is_y = jnp.logical_and(hx == sx, hy != sy)
    is_d = jnp.logical_and(hx != sx, hy != sy)
    partner = (hi * PAIR + (1 - lo), rep)
    my_q = xor(hi, mirror(rep, nrep), nrep)
    owner = (rep * PAIR + lo, my_q)
    moves = jnp.logical_or(owner[0] != row, owner[1] != rep)
    pieces = nrep * SPLIT
    grain = rows // pieces

    def ordered(i):
        place = 0
        for r in range(nrep):
            by_distance = sorted((k for k in range(nrep) if k != r), key=lambda k: (-abs(k - r), k))
            place = place + jnp.where(rep == r, by_distance[i], 0)
        return place

    far = [ordered(i) for i in range(nrep - 1)]

    barrier = pltpu.get_barrier_semaphore()

    def greet(device):
        pl.semaphore_signal(barrier, inc=1, device_id=device, device_id_type=MESH)

    for d in range(1, nrow):
        greet(((row + d) % nrow, rep))
    for d in range(1, nrep):
        greet((row, (rep + d) % nrep))

    for k in range(nrep):
        @pl.when(jnp.logical_or(hi != rep, rep != k))
        def _():
            greet((rep * PAIR + lo, k))
            greet((k * PAIR + lo, hi))

    def own_copy(c, k):
        return pltpu.make_async_copy(
            feat_hbm.at[pl.ds(k * grain, grain), pl.ds(c * lanes, lanes)],
            src.at[c, lo * pieces + k], own_sem.at[c, k],
        )

    @pl.when(is_src)
    def _():
        for c in range(slices):
            for k in range(pieces):
                own_copy(c, k).start()

    small = [
        pltpu.make_async_copy(a, b, small_sem.at[i])
        for i, (a, b) in enumerate((
            (blocks_hbm, blocks), (count_hbm, count), (deg_hbm, deg),
            (wself_hbm, wself), (wneigh_hbm, wneigh), (cot_hbm, cot),
        ))
    ]
    for copy in small:
        copy.start()
    tile_copies = [
        pltpu.make_async_copy(tiles_hbm.at[j], tiles.at[j], tile_sem.at[j]) for j in range(here)
    ]
    for copy in tile_copies:
        copy.start()
    feat_copy = pltpu.make_async_copy(
        feat_hbm.at[pl.ds(pl.multiple_of(rep * share, share), share)], my_feat, feat_sem
    )
    feat_copy.start()

    pl.semaphore_wait(barrier, nrow - 1 + nrep - 1 + 2 * (nrep - is_src.astype(jnp.int32)))

    def hop(c, k, i, h):
        at = src.at[c, lo * pieces + k]
        return remote(at, at, p1s.at[c, k, i], p1r.at[c, k], (h * PAIR + lo, rep))

    def x_peer():
        return hy * PAIR + (1 - hx)

    def y_peer(d):
        return ((hy + d) % ny) * PAIR + hx

    def to_partner(c, k):
        at = src.at[c, lo * pieces + k]
        return remote(at, at, p1ps.at[c, k], p1pr.at[c, k], partner)

    def from_partner(c, k):
        at = src.at[c, (1 - lo) * pieces + k]
        return remote(at, at, p1ps.at[c, k], p1pr.at[c, k], partner)

    first, second = list(range(pieces // 2)), list(range(pieces // 2, pieces))

    @pl.when(is_src)
    def _():
        for c in range(slices):
            for k in range(pieces):
                own_copy(c, k).wait()
            for kx, ky in zip(first + second, second + first):
                hop(c, kx, 0, x_peer()).start()
                for d in range(1, ny):
                    hop(c, ky, d, y_peer(d)).start()
            for k in range(pieces):
                to_partner(c, k).start()

    for copy in small:
        copy.wait()
    side = keys.shape[-1]
    at_row = lax.broadcasted_iota(jnp.int32, (side, side), 0)
    at_col = lax.broadcasted_iota(jnp.int32, (side, side), 1)
    for j in range(here):
        keys[...] = jnp.full(keys.shape, -1, jnp.int32)
        keys[0:1, 0:slots] = blocks[j, 0:1, :] * nblk + blocks[j, 1:2, :]
        line = jnp.broadcast_to(keys[0:1, :], (side, side))
        column = line.T
        before = jnp.where(jnp.logical_and(column == line, at_row < at_col), at_row + 1, 0)
        latest = jnp.where(jnp.logical_and(column == at_col, at_row < count[j]), at_row + 1, 0)
        tab_v[2 * j : 2 * j + 1, :] = jnp.max(before, axis=0, keepdims=True)
        tab_v[2 * j + 1 : 2 * j + 2, :] = jnp.max(latest, axis=0, keepdims=True)
    tab_copy = pltpu.make_async_copy(tab_v, tab_s, tab_sem)
    tab_copy.start()
    run = deg.shape[1]
    for b in range(rows // run):
        line = jnp.broadcast_to(deg[b : b + 1, :].astype(F32), (run, run))
        deg_col[pl.ds(b * run, run), :] = line.T
    tab_copy.wait()

    for j in range(here):
        tile_copies[j].wait()
        runs[0] = jnp.zeros((tile, tile), F32)

        def add(slot, carry):
            runs[slot + 1] = tiles[j, slot].astype(F32) + runs[tab_s[2 * j, slot]]
            return carry

        lax.fori_loop(0, slots, add, 0)

        def place(b, carry):
            for c in range(nblk):
                block = runs[tab_s[2 * j + 1, b * nblk + c]]
                adj[j, pl.ds(pl.multiple_of(b * tile, tile), tile), c * tile : (c + 1) * tile] = block.astype(BF16)
            return carry

        lax.fori_loop(0, nblk, place, 0)

    def relay(c):
        @pl.when(is_x)
        def _():
            for k in first + second:
                hop(c, k, 0, hi).wait_recv()
                if k in first:
                    for d in range(1, ny):
                        hop(c, k, d, y_peer(d)).start()
                to_partner(c, k).start()

        @pl.when(is_y)
        def _():
            for k in second + first:
                hop(c, k, 0, hi).wait_recv()
                if k in second:
                    hop(c, k, 0, x_peer()).start()
                to_partner(c, k).start()

        @pl.when(is_d)
        def _():
            for pair in zip(first, second):
                for k in pair:
                    hop(c, k, 0, hi).wait_recv()
                    to_partner(c, k).start()

        for k in range(pieces):
            from_partner(c, k).wait_recv()

    def partial(c, at, n):
        total = jnp.zeros((n, lanes), F32)
        for j in range(here):
            a = adj[j, pl.ds(pl.multiple_of(at, n), n), :]
            f = src[c, pl.ds(j * pieces, pieces)].reshape(rows, lanes)
            total = total + jnp.dot(a, f, preferred_element_type=F32)
        return total

    last = slices - 1
    step = share // PARTS

    def send_dagg(c, to, i):
        at = dagg.at[c, rep, pl.ds(i * step, step)]
        return remote(at, at, cs.at[c, to, i], cr.at[c, rep, i], (row, to))

    tail = cut(lanes, TAIL)

    def send_late(n, to):
        f0, fs = tail[n]
        at = late.at[rep, pl.ds(f0, fs)]
        return remote(at, at, ts.at[n, to], tr.at[n, rep], (row, to))

    def get_late(n, k):
        f0, fs = tail[n]
        at = late.at[k, pl.ds(f0, fs)]
        return remote(at, at, ts.at[n, k], tr.at[n, k], (row, k))

    def get_dagg(c, k, i):
        at = dagg.at[c, k, pl.ds(i * step, step)]
        return remote(at, at, cs.at[c, k, i], cr.at[c, k, i], (row, k))

    def send_part(c, to):
        return remote(
            part.at[c, to], part_in.at[c, rep], bs.at[c, to], br.at[c, rep], (row, to)
        )

    def get_part(c, k):
        return remote(part_in.at[c, k], part_in.at[c, k], bs.at[c, k], br.at[c, k], (row, k))

    def send_step(to, i):
        steps = pl.ds(i * step, step)
        return remote(
            part.at[last, to, steps], part_in.at[last, rep, steps], es.at[to, i], er.at[rep, i], (row, to)
        )

    def get_step(k, i):
        at = part_in.at[last, k, pl.ds(i * step, step)]
        return remote(at, at, es.at[k, i], er.at[k, i], (row, k))

    def finish_sums():
        @pl.when(is_src)
        def _():
            for c in range(slices):
                for k in range(pieces):
                    hop(c, k, 0, x_peer()).wait_send()
                    for d in range(1, ny):
                        hop(c, k, d, y_peer(d)).wait_send()

        @pl.when(is_x)
        def _():
            for c in range(slices):
                for k in first:
                    for d in range(1, ny):
                        hop(c, k, d, y_peer(d)).wait_send()

        @pl.when(is_y)
        def _():
            for c in range(slices):
                for k in second:
                    hop(c, k, 0, x_peer()).wait_send()

        for c in range(slices):
            for k in range(pieces):
                to_partner(c, k).wait_send()
        for to in far:
            for c in range(last):
                send_part(c, to).wait_send()
            for i in range(PARTS):
                send_step(to, i).wait_send()

    def finish_gather():
        for to in far:
            for i in range(PARTS):
                send_dagg(0, to, i).wait_send()
            for n in range(len(tail)):
                send_late(n, to).wait_send()
        for d in range(1, nrow):
            send_w1(d).wait_send()
        for q in range(nrep):
            send_pair(0, q).wait_send()

    def finish_rest():
        for e in range(1, half):
            send_plane(0, e).wait_send()

        @pl.when(moves)
        def _():
            to_owner(0).wait_send()

        for n in range(len(tail)):
            for q in range(nrep):
                send_late_pair(n, q).wait_send()
            if n in DIRECT:
                for to in far:
                    straight_to(n, to).wait_send()

                @pl.when(jnp.logical_not(is_src))
                def _():
                    straight_to(n, rep).wait_send()
            else:
                for e in range(1, half):
                    send_late_plane(n, e).wait_send()

                @pl.when(moves)
                def _():
                    late_to_owner(n).wait_send()

        for d in range(1, nrep):
            send_w2(d).wait_send()
        for e in range(half):
            if e > 0:
                send_w3(e).wait_send()
            share_w3(e).wait_send()

    for c in range(slices):
        relay(c)
        if c < last:
            for to in far:
                part[c, to] = partial(c, to * share, share).astype(BF16)
                send_part(c, to).start()
        else:
            for i in range(PARTS):
                for to in far:
                    part[c, to, pl.ds(i * step, step)] = partial(c, to * share + i * step, step).astype(BF16)
                    send_step(to, i).start()
        mine[c] = partial(c, rep * share, share)
    feat_copy.wait()
    base[...] = jnp.dot(my_feat[...], wself[...], preferred_element_type=F32)

    for c in range(last):
        for k in far:
            get_part(c, k).wait_recv()
            mine[c] = mine[c] + part_in[c, k].astype(F32)
    for i in range(PARTS):
        at = pl.ds(i * step, step)
        degree = deg_col[pl.ds(pl.multiple_of(rep * share + i * step, step), step), :]
        total = mine[last, at]
        for k in far:
            get_step(k, i).wait_recv()
            total = total + part_in[last, k, at].astype(F32)
        sums = [mine[c, at] for c in range(last)] + [total]
        agg = jnp.concatenate([(s / degree).astype(BF16) for s in sums], axis=1)
        agg_all[at] = agg
        pre = base[at] + jnp.dot(agg, wneigh[...], preferred_element_type=F32)
        sig = jax.nn.sigmoid(pre)
        gpre = (cot[at].astype(F32) * sig * (1.0 + pre * (1.0 - sig))).astype(BF16)
        gpre_all[at] = gpre
        back_t = lax.dot_general(gpre, wneigh[...], (((1,), (1,)), ((), ())), preferred_element_type=F32)
        for c in range(slices):
            dagg[c, rep, at] = (back_t[:, c * lanes : (c + 1) * lanes] / degree).astype(BF16)
        for to in far:
            send_dagg(0, to, i).start()
        out[at] = (pre * sig).astype(BF16)
    late[rep] = dagg[last, rep].T
    for n in range(len(tail)):
        for to in far:
            send_late(n, to).start()

    gpre = gpre_all[...]
    ws = lax.dot_general(my_feat[...], gpre, (((0,), (0,)), ((), ())), preferred_element_type=F32)
    wn = lax.dot_general(agg_all[...], gpre, (((0,), (0,)), ((), ())), preferred_element_type=F32)
    piece = wpart.shape[1]
    wpart[pl.ds(0, half)] = ws.astype(BF16).reshape(half, piece, width)
    wpart[pl.ds(half, half)] = wn.astype(BF16).reshape(half, piece, width)

    def send_w1(d):
        to = (row + d) % nrow
        return remote(wpart.at[to], wrow_in.at[d - 1], w1s.at[d - 1], w1r.at[d - 1], (to, rep))

    for d in range(1, nrow):
        send_w1(d).start()
    base[...] = lax.dot_general(gpre, wself[...], (((1,), (1,)), ((), ())), preferred_element_type=F32)

    unit = max(share, 128)
    per_unit = unit // share

    def send_pair(c, q):
        return remote(
            terms.at[c, (1 - lo) * nrep + q], pair_in.at[c, q], d0s.at[c, q], d0r.at[c, q], partner
        )

    def send_plane(c, e):
        return remote(
            summed.at[c, e - 1], plane_in.at[c, e - 1], d1s.at[c, e - 1], d1r.at[c, e - 1],
            (xor(hi, e, half) * PAIR + lo, rep),
        )

    def to_owner(c):
        return remote(back.at[c], back_in.at[c], d2s.at[c], d2r.at[c], owner)

    def straight_to(n, q):
        f0, fs = tail[n]
        return remote(
            straight.at[q, pl.ds(f0, fs)], straight_in.at[hi, pl.ds(f0, fs)],
            d3s.at[n, q], d3r.at[n, hi], (rep * PAIR + lo, q),
        )

    def straight_from(n, k):
        f0, fs = tail[n]
        at = straight_in.at[k, pl.ds(f0, fs)]
        return remote(at, at, d3s.at[n, k], d3r.at[n, k], (k * PAIR + lo, hi))

    def send_late_pair(n, q):
        f0, fs = tail[n]
        return remote(
            terms.at[last, (1 - lo) * nrep + q, pl.ds(f0, fs)], pair_in.at[last, q, pl.ds(f0, fs)],
            t0s.at[n, q], t0r.at[n, q], partner,
        )

    def gain(sums, f0, fs, left, k, start, emit):
        for j in (1 - lo, lo):
            slot = 0 if j is lo else 1
            for u in range(rows // unit):
                a = adj[j, pl.ds(pl.multiple_of(k * share, share), share), u * unit : (u + 1) * unit]
                t = jnp.dot(left, a, preferred_element_type=F32)
                if not start:
                    t = t + sums[slot, u, f0 : f0 + fs, :]
                if emit is None:
                    sums[slot, u, f0 : f0 + fs, :] = t
                    continue
                t = t.astype(BF16)
                for v in range(per_unit):
                    emit(j, u * per_unit + v, t[:, v * share : (v + 1) * share])

    def emit_early(j, q, value):
        terms[0, j * nrep + q] = value
        if j is not lo:
            send_pair(0, q).start()

    def emit_late(n):
        f0, fs = tail[n]

        def emit(j, q, value):
            terms[last, j * nrep + q, f0 : f0 + fs, :] = value
            if j is not lo:
                send_late_pair(n, q).start()

        return emit

    def make_own():
        gain(acc, 0, lanes, dagg[0, rep].T, rep, True, None)
        gain(late_acc, 0, lanes, late[rep], rep, True, None)

    def make_early():
        near = far[::-1]
        for k in near:
            for i in range(PARTS):
                get_dagg(0, k, i).wait_recv()
            gain(acc, 0, lanes, dagg[0, k].T, k, False, emit_early if k is near[-1] else None)

    def make_late(n):
        f0, fs = tail[n]
        near = far[::-1]
        for k in near:
            get_late(n, k).wait_recv()
            gain(late_acc, f0, fs, late[k, f0 : f0 + fs, :], k, False, emit_late(n) if k is near[-1] else None)

    def send_late_plane(n, e):
        f0, fs = tail[n]
        at = (last, e - 1, pl.ds(f0, fs))
        return remote(
            summed.at[at], plane_in.at[at], t1s.at[n, e - 1], t1r.at[n, e - 1],
            (xor(hi, e, half) * PAIR + lo, rep),
        )

    def late_to_owner(n):
        f0, fs = tail[n]
        at = (last, pl.ds(f0, fs))
        return remote(back.at[at], back_in.at[at], t2s.at[n], t2r.at[n], owner)

    def add_late_plane(n):
        f0, fs = tail[n]
        both = back_sum[n + 1]
        for e in range(1, half):
            send_late_plane(n, e).wait_recv()
            both = both + plane_in[last, e - 1, f0 : f0 + fs, :].astype(F32)
        back[last, f0 : f0 + fs, :] = both.astype(BF16)

        @pl.when(moves)
        def _():
            late_to_owner(n).start()

    def add_late_pair(n):
        f0, fs = tail[n]
        if n not in DIRECT:
            for e in list(range(half - 1, 0, -1)) + [0]:
                q = xor(xor(hi, e, half), mirror(rep, nrep), nrep)
                send_late_pair(n, q).wait_recv()
                both = terms[last, lo * nrep + q, f0 : f0 + fs, :].astype(F32)
                both = both + pair_in[last, q, f0 : f0 + fs, :].astype(F32)
                if e > 0:
                    summed[last, e - 1, f0 : f0 + fs, :] = both.astype(BF16)
                    send_late_plane(n, e).start()
                else:
                    back_sum[n + 1] = both
            return
        for q in far + [rep]:
            send_late_pair(n, q).wait_recv()
            both = terms[last, lo * nrep + q, f0 : f0 + fs, :].astype(F32)
            both = (both + pair_in[last, q, f0 : f0 + fs, :].astype(F32)).astype(BF16)
            straight[q, f0 : f0 + fs, :] = both
            if q is rep:
                @pl.when(jnp.logical_not(is_src))
                def _():
                    straight_to(n, q).start()

                @pl.when(is_src)
                def _():
                    straight_in[hi, f0 : f0 + fs, :] = both
            else:
                straight_to(n, q).start()

    def add_pair(c):
        for e in list(range(half - 1, 0, -1)) + [0]:
            q = xor(xor(hi, e, half), mirror(rep, nrep), nrep)
            send_pair(c, q).wait_recv()
            both = terms[c, lo * nrep + q].astype(F32) + pair_in[c, q].astype(F32)
            if e > 0:
                summed[c, e - 1] = both.astype(BF16)
                send_plane(c, e).start()
            else:
                back_sum[c] = both

    def add_plane(c):
        both = back_sum[c]
        for e in range(1, half):
            send_plane(c, e).wait_recv()
            both = both + plane_in[c, e - 1].astype(F32)
        back[c] = both.astype(BF16)

        @pl.when(moves)
        def _():
            to_owner(c).start()

    back_sum = {}
    def send_w2(d):
        return remote(
            wrep_in.at[rep], wrep_in.at[rep], w2s.at[d - 1], w2r.at[d - 1], (row, (rep + d) % nrep)
        )

    def send_w3(e):
        return remote(
            wall.at[row], wall.at[row], w3s.at[e - 1], w3r.at[e - 1], (xor(hi, e, half) * PAIR + lo, rep)
        )

    def get_w3(e):
        at = wall.at[xor(hi, e, half) * PAIR + lo]
        return remote(at, at, w3s.at[e - 1], w3r.at[e - 1], (row, rep))

    def share_w3(e):
        at = wall.at[xor(hi, e, half) * PAIR + lo]
        return remote(at, at, w3ps.at[e], w3pr.at[e], partner)

    def shared_w3(e):
        at = wall.at[xor(hi, e, half) * PAIR + (1 - lo)]
        return remote(at, at, w3ps.at[e], w3pr.at[e], partner)

    def reduce_rows():
        wsum = wpart[row].astype(F32)
        for d in range(1, nrow):
            send_w1(d).wait_recv()
            wsum = wsum + wrow_in[d - 1].astype(F32)
        wrep_in[rep] = wsum.astype(BF16)
        for d in range(1, nrep):
            send_w2(d).start()

    def reduce_reps():
        for d in range(1, nrep):
            remote(
                wrep_in.at[rep], wrep_in.at[(rep + nrep - d) % nrep], w2s.at[d - 1], w2r.at[d - 1], (row, rep)
            ).wait_recv()
        wsum = wrep_in[0].astype(F32)
        for k in range(1, nrep):
            wsum = wsum + wrep_in[k].astype(F32)
        wall[row] = wsum.astype(BF16)
        for e in range(1, half):
            send_w3(e).start()
        share_w3(0).start()

    make_own()
    finish_sums()
    make_early()
    add_pair(0)
    reduce_rows()
    for n in range(len(tail)):
        make_late(n)
        add_late_pair(n)
    finish_gather()
    for c in range(last):
        add_plane(c)
    reduce_reps()
    for n in range(len(tail)):
        if n not in DIRECT:
            add_late_plane(n)
    for e in range(1, half):
        get_w3(e).wait_recv()
        share_w3(e).start()

    for c in range(last):
        cols = slice(c * lanes, (c + 1) * lanes)

        @pl.when(moves)
        def _():
            to_owner(c).wait_recv()
            gfeat[:, cols] = (base[:, cols] + back_in[c].astype(F32).T).astype(BF16)

        @pl.when(jnp.logical_not(moves))
        def _():
            gfeat[:, cols] = (base[:, cols] + back[c].astype(F32).T).astype(BF16)

    for n, (f0, fs) in enumerate(tail):
        if n not in DIRECT:
            cols = slice(last * lanes + f0, last * lanes + f0 + fs)

            @pl.when(moves)
            def _():
                late_to_owner(n).wait_recv()
                gfeat[:, cols] = (base[:, cols] + back_in[last, f0 : f0 + fs, :].astype(F32).T).astype(BF16)

            @pl.when(jnp.logical_not(moves))
            def _():
                gfeat[:, cols] = (base[:, cols] + back[last, f0 : f0 + fs, :].astype(F32).T).astype(BF16)

            continue
        for k in range(half):
            @pl.when(jnp.logical_or(rep != hi, hi != k))
            def _():
                straight_from(n, k).wait_recv()

        both = jnp.zeros((fs, share), F32)
        for k in range(half):
            both = both + straight_in[k, f0 : f0 + fs, :].astype(F32)
        both = both.astype(BF16).astype(F32)
        at = last * lanes + f0
        gfeat[:, at : at + fs] = (base[:, at : at + fs] + both.T).astype(BF16)
    for e in range(half):
        shared_w3(e).wait_recv()
    finish_rest()


def close_kernel(out_in, wall, gfeat_in, out, gself, gneigh, gfeat):
    half = wall.shape[0] // 2
    out[...] = out_in[...]
    gfeat[...] = gfeat_in[...]
    gself[...] = wall[pl.ds(0, half)].reshape(gself.shape).astype(F32)
    gneigh[...] = wall[pl.ds(half, half)].reshape(gneigh.shape).astype(F32)


def body(
    nrow, nrep,
    features, weight_self, weight_neigh, degrees, tile_values, tile_blocks, tile_count, cotangent,
):
    rows, width = features.shape
    here, slots, tile = tile_values.shape[1], tile_values.shape[2], tile_values.shape[-1]
    share = rows // nrep
    half = nrow // PAIR
    ny = half // PAIR
    piece = 2 * width // nrow
    lanes = 128
    slices = width // lanes
    pieces = nrep * SPLIT
    unit = max(share, 128)
    nt = len(TAIL)
    assert slices == 2 and here == PAIR and half == nrep and (rows // tile) ** 2 <= 128 and slots <= 128
    sems = pltpu.SemaphoreType.DMA
    vmem = pl.BlockSpec(memory_space=pltpu.VMEM)
    anywhere = pl.BlockSpec(memory_space=pltpu.HBM)

    def buf(*shape):
        return pltpu.VMEM(shape, BF16)

    out, wall, gfeat = pl.pallas_call(
        functools.partial(layer_kernel, nrow, nrep, here),
        out_shape=(
            jax.ShapeDtypeStruct((share, width), BF16),
            jax.ShapeDtypeStruct((nrow, piece, width), BF16),
            jax.ShapeDtypeStruct((share, width), BF16),
        ),
        in_specs=[anywhere] * 8,
        out_specs=(vmem,) * 3,
        scratch_shapes=[
            buf(width, width), buf(width, width),
            pltpu.VMEM((rows // tile, tile), jnp.int32),
            buf(share, width),
            pltpu.VMEM((here, 2, slots), jnp.int32),
            pltpu.SMEM((here,), jnp.int32),
            buf(here, slots, tile, tile),
            pltpu.VMEM((slots + 1, tile, tile), F32),
            buf(here, rows, rows),
            pltpu.VMEM((8, 128), jnp.int32),
            pltpu.VMEM((8, 128), jnp.int32),
            pltpu.SMEM((8, 128), jnp.int32),
            buf(share, width),
            buf(slices, here * pieces, rows // pieces, lanes),
            pltpu.VMEM((slices, share, lanes), F32),
            buf(slices, nrep, share, lanes),
            buf(slices, nrep, share, lanes),
            buf(share, width),
            buf(share, width),
            buf(slices, nrep, share, lanes),
            buf(nrep, lanes, share),
            pltpu.VMEM((here, rows // unit, lanes, unit), F32),
            pltpu.VMEM((here, rows // unit, lanes, unit), F32),
            buf(slices, nrow, lanes, share),
            buf(slices, nrep, lanes, share),
            buf(slices, half - 1, lanes, share),
            buf(slices, half - 1, lanes, share),
            buf(slices, lanes, share),
            buf(slices, lanes, share),
            buf(nrep, lanes, share),
            buf(half, lanes, share),
            buf(nrow, piece, width),
            buf(nrow - 1, piece, width),
            buf(nrep, piece, width),
            pltpu.VMEM((share, width), F32),
            pltpu.VMEM((rows, tile), F32),
            sems((6,)), sems((here,)), sems, sems, sems((slices, pieces)),
            sems((slices, pieces, ny)), sems((slices, pieces)), sems((slices, pieces)), sems((slices, pieces)),
            sems((slices, nrep)), sems((slices, nrep)),
            sems((nrep, PARTS)), sems((nrep, PARTS)),
            sems((slices, nrep, PARTS)), sems((slices, nrep, PARTS)),
            sems((nrow - 1,)), sems((nrow - 1,)),
            sems((nrep - 1,)), sems((nrep - 1,)),
            sems((half - 1,)), sems((half - 1,)), sems((half,)), sems((half,)),
            sems((slices, nrep)), sems((slices, nrep)),
            sems((slices, half - 1)), sems((slices, half - 1)),
            sems((slices,)), sems((slices,)),
            sems((nt, nrep)), sems((nt, half)), sems((nt, nrep)), sems((nt, nrep)),
            sems((nt, nrep)), sems((nt, nrep)),
            sems((nt, half - 1)), sems((nt, half - 1)), sems((nt,)), sems((nt,)),
        ],
        compiler_params=pltpu.CompilerParams(
            collective_id=0, has_side_effects=True, vmem_limit_bytes=44 * 2**20
        ),
        name="layer",
    )(*(
        pltpu.with_memory_space_constraint(x, pltpu.HBM)
        for x in (
            features, weight_self, weight_neigh, degrees.reshape(rows // tile, tile), cotangent,
            tile_values[0], tile_blocks.transpose(0, 1, 3, 2)[0], tile_count[0],
        )
    ))
    out, grad_self, grad_neigh, gfeat = pl.pallas_call(
        close_kernel,
        out_shape=(
            jax.ShapeDtypeStruct((share, width), BF16),
            jax.ShapeDtypeStruct((width, width), F32),
            jax.ShapeDtypeStruct((width, width), F32),
            jax.ShapeDtypeStruct((share, width), BF16),
        ),
        in_specs=[vmem] * 3,
        out_specs=(vmem,) * 4,
        compiler_params=pltpu.CompilerParams(vmem_limit_bytes=8 * 2**20),
        name="close",
    )(out, wall, gfeat)
    return out, grad_self, grad_neigh, gfeat


def solution(mesh):
    in_specs = (
        P("row", None),
        P(),
        P(),
        P("row"),
        P("row", "rep", None, None, None),
        P("row", "rep", None, None),
        P("row", "rep"),
        P(("row", "rep"), None),
    )
    out_specs = (P(("row", "rep"), None), P(), P(), P(("row", "rep"), None))
    run = functools.partial(body, mesh.shape["row"], mesh.shape["rep"])
    return jax.shard_map(run, mesh=mesh, in_specs=in_specs, out_specs=out_specs, check_vma=False)
```

```python
import functools

import jax
import jax.numpy as jnp
from jax import lax
from jax.experimental import pallas as pl
from jax.experimental.pallas import tpu as pltpu
from jax.sharding import PartitionSpec as P

MESH = pl.DeviceIdType.MESH
F32 = jnp.float32
BF16 = jnp.bfloat16
PAIR = 2
PARTS = 4
SPLIT = 1
TAIL = (5, 3)
DIRECT = (1,)


def remote(src, dst, send, recv, device):
    return pltpu.make_async_remote_copy(
        src_ref=src, dst_ref=dst, send_sem=send, recv_sem=recv, device_id=device, device_id_type=MESH
    )


def cut(width, shares):
    spans, at = [], 0
    for s in shares:
        spans.append((at, width * s // sum(shares)))
        at += width * s // sum(shares)
    assert at == width
    return spans


def bits_of(n):
    return (n - 1).bit_length()


def xor(a, b, n):
    total = 0
    for k in range(bits_of(n)):
        w = 2**k
        total = total + ((a // w + b // w) % 2) * w
    return total


def mirror(a, n):
    total = 0
    top = bits_of(n)
    for k in range(top):
        total = total + ((a // 2**k) % 2) * 2 ** (top - 1 - k)
    return total


def layer_kernel(
    nrow, nrep, here,
    feat_hbm, wself_hbm, wneigh_hbm, deg_hbm, cot_hbm, tiles_hbm, blocks_hbm, count_hbm,
    out, wall, gfeat,
    wself, wneigh, deg, cot, blocks, count, tiles, runs, adj, keys, tab_v, tab_s, my_feat, src, mine, part, part_in, agg_all, gpre_all,
    dagg, late, acc, late_acc, terms, pair_in, summed, plane_in, back, back_in, straight, straight_in,
    wpart, wrow_in, wrep_in, base, deg_col,
    small_sem, tile_sem, tab_sem, feat_sem, own_sem,
    p1s, p1r, p1ps, p1pr, bs, br, es, er, cs, cr, w1s, w1r, w2s, w2r, w3s, w3r, w3ps, w3pr,
    d0s, d0r, d1s, d1r, d2s, d2r, d3s, d3r, ts, tr, t0s, t0r, t1s, t1r, t2s, t2r,
):
    row, rep = lax.axis_index("row"), lax.axis_index("rep")
    rows, width = feat_hbm.shape
    lanes = src.shape[-1]
    slices = width // lanes
    share = rows // nrep
    half = nrow // PAIR
    tile = tiles.shape[-1]
    slots = tiles.shape[1]
    nblk = rows // tile
    hi, lo = row // PAIR, row % PAIR
    hx, hy = hi % PAIR, hi // PAIR
    ny = half // PAIR
    sx, sy = rep % PAIR, rep // PAIR
    is_src = hi == rep
    is_x = jnp.logical_and(hy == sy, hx != sx)
    is_y = jnp.logical_and(hx == sx, hy != sy)
    is_d = jnp.logical_and(hx != sx, hy != sy)
    partner = (hi * PAIR + (1 - lo), rep)
    my_q = xor(hi, mirror(rep, nrep), nrep)
    owner = (rep * PAIR + lo, my_q)
    moves = jnp.logical_or(owner[0] != row, owner[1] != rep)
    pieces = nrep * SPLIT
    grain = rows // pieces

    def ordered(i):
        place = 0
        for r in range(nrep):
            by_distance = sorted((k for k in range(nrep) if k != r), key=lambda k: (-abs(k - r), k))
            place = place + jnp.where(rep == r, by_distance[i], 0)
        return place

    far = [ordered(i) for i in range(nrep - 1)]

    barrier = pltpu.get_barrier_semaphore()

    def greet(device):
        pl.semaphore_signal(barrier, inc=1, device_id=device, device_id_type=MESH)

    for d in range(1, nrow):
        greet(((row + d) % nrow, rep))
    for d in range(1, nrep):
        greet((row, (rep + d) % nrep))

    for k in range(nrep):
        @pl.when(jnp.logical_or(hi != rep, rep != k))
        def _():
            greet((rep * PAIR + lo, k))
            greet((k * PAIR + lo, hi))

    def own_copy(c, k):
        return pltpu.make_async_copy(
            feat_hbm.at[pl.ds(k * grain, grain), pl.ds(c * lanes, lanes)],
            src.at[c, lo * pieces + k], own_sem.at[c, k],
        )

    @pl.when(is_src)
    def _():
        for c in range(slices):
            for k in range(pieces):
                own_copy(c, k).start()

    small = [
        pltpu.make_async_copy(a, b, small_sem.at[i])
        for i, (a, b) in enumerate((
            (blocks_hbm, blocks), (count_hbm, count), (deg_hbm, deg),
            (wself_hbm, wself), (wneigh_hbm, wneigh), (cot_hbm, cot),
        ))
    ]
    for copy in small:
        copy.start()
    tile_copies = [
        pltpu.make_async_copy(tiles_hbm.at[j], tiles.at[j], tile_sem.at[j]) for j in range(here)
    ]
    for copy in tile_copies:
        copy.start()
    feat_copy = pltpu.make_async_copy(
        feat_hbm.at[pl.ds(pl.multiple_of(rep * share, share), share)], my_feat, feat_sem
    )
    feat_copy.start()

    pl.semaphore_wait(barrier, nrow - 1 + nrep - 1 + 2 * (nrep - is_src.astype(jnp.int32)))

    def hop(c, k, i, h):
        at = src.at[c, lo * pieces + k]
        return remote(at, at, p1s.at[c, k, i], p1r.at[c, k], (h * PAIR + lo, rep))

    def x_peer():
        return hy * PAIR + (1 - hx)

    def y_peer(d):
        return ((hy + d) % ny) * PAIR + hx

    def to_partner(c, k):
        at = src.at[c, lo * pieces + k]
        return remote(at, at, p1ps.at[c, k], p1pr.at[c, k], partner)

    def from_partner(c, k):
        at = src.at[c, (1 - lo) * pieces + k]
        return remote(at, at, p1ps.at[c, k], p1pr.at[c, k], partner)

    first, second = list(range(pieces // 2)), list(range(pieces // 2, pieces))

    @pl.when(is_src)
    def _():
        for c in range(slices):
            for k in range(pieces):
                own_copy(c, k).wait()
            for kx, ky in zip(first + second, second + first):
                hop(c, kx, 0, x_peer()).start()
                for d in range(1, ny):
                    hop(c, ky, d, y_peer(d)).start()
            for k in range(pieces):
                to_partner(c, k).start()

    for copy in small:
        copy.wait()
    side = keys.shape[-1]
    at_row = lax.broadcasted_iota(jnp.int32, (side, side), 0)
    at_col = lax.broadcasted_iota(jnp.int32, (side, side), 1)
    for j in range(here):
        keys[...] = jnp.full(keys.shape, -1, jnp.int32)
        keys[0:1, 0:slots] = blocks[j, 0:1, :] * nblk + blocks[j, 1:2, :]
        line = jnp.broadcast_to(keys[0:1, :], (side, side))
        column = line.T
        before = jnp.where(jnp.logical_and(column == line, at_row < at_col), at_row + 1, 0)
        latest = jnp.where(jnp.logical_and(column == at_col, at_row < count[j]), at_row + 1, 0)
        tab_v[2 * j : 2 * j + 1, :] = jnp.max(before, axis=0, keepdims=True)
        tab_v[2 * j + 1 : 2 * j + 2, :] = jnp.max(latest, axis=0, keepdims=True)
    tab_copy = pltpu.make_async_copy(tab_v, tab_s, tab_sem)
    tab_copy.start()
    run = deg.shape[1]
    for b in range(rows // run):
        line = jnp.broadcast_to(deg[b : b + 1, :].astype(F32), (run, run))
        deg_col[pl.ds(b * run, run), :] = line.T
    tab_copy.wait()

    for j in range(here):
        tile_copies[j].wait()
        runs[0] = jnp.zeros((tile, tile), F32)

        def add(slot, carry):
            runs[slot + 1] = tiles[j, slot].astype(F32) + runs[tab_s[2 * j, slot]]
            return carry

        lax.fori_loop(0, slots, add, 0)

        def place(b, carry):
            for c in range(nblk):
                block = runs[tab_s[2 * j + 1, b * nblk + c]]
                adj[j, pl.ds(pl.multiple_of(b * tile, tile), tile), c * tile : (c + 1) * tile] = block.astype(BF16)
            return carry

        lax.fori_loop(0, nblk, place, 0)

    def relay(c):
        @pl.when(is_x)
        def _():
            for k in first + second:
                hop(c, k, 0, hi).wait_recv()
                if k in first:
                    for d in range(1, ny):
                        hop(c, k, d, y_peer(d)).start()
                to_partner(c, k).start()

        @pl.when(is_y)
        def _():
            for k in second + first:
                hop(c, k, 0, hi).wait_recv()
                if k in second:
                    hop(c, k, 0, x_peer()).start()
                to_partner(c, k).start()

        @pl.when(is_d)
        def _():
            for pair in zip(first, second):
                for k in pair:
                    hop(c, k, 0, hi).wait_recv()
                    to_partner(c, k).start()

        for k in range(pieces):
            from_partner(c, k).wait_recv()

    def partial(c, at, n):
        total = jnp.zeros((n, lanes), F32)
        for j in range(here):
            a = adj[j, pl.ds(pl.multiple_of(at, n), n), :]
            f = src[c, pl.ds(j * pieces, pieces)].reshape(rows, lanes)
            total = total + jnp.dot(a, f, preferred_element_type=F32)
        return total

    last = slices - 1
    step = share // PARTS

    def send_dagg(c, to, i):
        at = dagg.at[c, rep, pl.ds(i * step, step)]
        return remote(at, at, cs.at[c, to, i], cr.at[c, rep, i], (row, to))

    tail = cut(lanes, TAIL)

    def send_late(n, to):
        f0, fs = tail[n]
        at = late.at[rep, pl.ds(f0, fs)]
        return remote(at, at, ts.at[n, to], tr.at[n, rep], (row, to))

    def get_late(n, k):
        f0, fs = tail[n]
        at = late.at[k, pl.ds(f0, fs)]
        return remote(at, at, ts.at[n, k], tr.at[n, k], (row, k))

    def get_dagg(c, k, i):
        at = dagg.at[c, k, pl.ds(i * step, step)]
        return remote(at, at, cs.at[c, k, i], cr.at[c, k, i], (row, k))

    def send_part(c, to):
        return remote(
            part.at[c, to], part_in.at[c, rep], bs.at[c, to], br.at[c, rep], (row, to)
        )

    def get_part(c, k):
        return remote(part_in.at[c, k], part_in.at[c, k], bs.at[c, k], br.at[c, k], (row, k))

    def send_step(to, i):
        steps = pl.ds(i * step, step)
        return remote(
            part.at[last, to, steps], part_in.at[last, rep, steps], es.at[to, i], er.at[rep, i], (row, to)
        )

    def get_step(k, i):
        at = part_in.at[last, k, pl.ds(i * step, step)]
        return remote(at, at, es.at[k, i], er.at[k, i], (row, k))

    def finish_sums():
        @pl.when(is_src)
        def _():
            for c in range(slices):
                for k in range(pieces):
                    hop(c, k, 0, x_peer()).wait_send()
                    for d in range(1, ny):
                        hop(c, k, d, y_peer(d)).wait_send()

        @pl.when(is_x)
        def _():
            for c in range(slices):
                for k in first:
                    for d in range(1, ny):
                        hop(c, k, d, y_peer(d)).wait_send()

        @pl.when(is_y)
        def _():
            for c in range(slices):
                for k in second:
                    hop(c, k, 0, x_peer()).wait_send()

        for c in range(slices):
            for k in range(pieces):
                to_partner(c, k).wait_send()
        for to in far:
            for c in range(last):
                send_part(c, to).wait_send()
            for i in range(PARTS):
                send_step(to, i).wait_send()

    def finish_gather():
        for to in far:
            for i in range(PARTS):
                send_dagg(0, to, i).wait_send()
            for n in range(len(tail)):
                send_late(n, to).wait_send()
        for d in range(1, nrow):
            send_w1(d).wait_send()
        for q in range(nrep):
            send_pair(0, q).wait_send()

    def finish_rest():
        for e in range(1, half):
            send_plane(0, e).wait_send()

        @pl.when(moves)
        def _():
            to_owner(0).wait_send()

        for n in range(len(tail)):
            for q in range(nrep):
                send_late_pair(n, q).wait_send()
            if n in DIRECT:
                for to in far:
                    straight_to(n, to).wait_send()

                @pl.when(jnp.logical_not(is_src))
                def _():
                    straight_to(n, rep).wait_send()
            else:
                for e in range(1, half):
                    send_late_plane(n, e).wait_send()

                @pl.when(moves)
                def _():
                    late_to_owner(n).wait_send()

        for d in range(1, nrep):
            send_w2(d).wait_send()
        for e in range(half):
            if e > 0:
                send_w3(e).wait_send()
            share_w3(e).wait_send()

    for c in range(slices):
        relay(c)
        if c < last:
            for to in far:
                part[c, to] = partial(c, to * share, share).astype(BF16)
                send_part(c, to).start()
        else:
            for i in range(PARTS):
                for to in far:
                    part[c, to, pl.ds(i * step, step)] = partial(c, to * share + i * step, step).astype(BF16)
                    send_step(to, i).start()
        mine[c] = partial(c, rep * share, share)
    feat_copy.wait()
    base[...] = jnp.dot(my_feat[...], wself[...], preferred_element_type=F32)

    for c in range(last):
        for k in far:
            get_part(c, k).wait_recv()
            mine[c] = mine[c] + part_in[c, k].astype(F32)
    for i in range(PARTS):
        at = pl.ds(i * step, step)
        degree = deg_col[pl.ds(pl.multiple_of(rep * share + i * step, step), step), :]
        total = mine[last, at]
        for k in far:
            get_step(k, i).wait_recv()
            total = total + part_in[last, k, at].astype(F32)
        sums = [mine[c, at] for c in range(last)] + [total]
        agg = jnp.concatenate([(s / degree).astype(BF16) for s in sums], axis=1)
        agg_all[at] = agg
        pre = base[at] + jnp.dot(agg, wneigh[...], preferred_element_type=F32)
        sig = jax.nn.sigmoid(pre)
        gpre = (cot[at].astype(F32) * sig * (1.0 + pre * (1.0 - sig))).astype(BF16)
        gpre_all[at] = gpre
        back_t = lax.dot_general(gpre, wneigh[...], (((1,), (1,)), ((), ())), preferred_element_type=F32)
        for c in range(slices):
            dagg[c, rep, at] = (back_t[:, c * lanes : (c + 1) * lanes] / degree).astype(BF16)
        for to in far:
            send_dagg(0, to, i).start()
        out[at] = (pre * sig).astype(BF16)
    late[rep] = dagg[last, rep].T
    for n in range(len(tail)):
        for to in far:
            send_late(n, to).start()

    gpre = gpre_all[...]
    ws = lax.dot_general(my_feat[...], gpre, (((0,), (0,)), ((), ())), preferred_element_type=F32)
    wn = lax.dot_general(agg_all[...], gpre, (((0,), (0,)), ((), ())), preferred_element_type=F32)
    piece = wpart.shape[1]
    wpart[pl.ds(0, half)] = ws.astype(BF16).reshape(half, piece, width)
    wpart[pl.ds(half, half)] = wn.astype(BF16).reshape(half, piece, width)

    def send_w1(d):
        to = (row + d) % nrow
        return remote(wpart.at[to], wrow_in.at[d - 1], w1s.at[d - 1], w1r.at[d - 1], (to, rep))

    for d in range(1, nrow):
        send_w1(d).start()
    base[...] = lax.dot_general(gpre, wself[...], (((1,), (1,)), ((), ())), preferred_element_type=F32)

    unit = max(share, 128)
    per_unit = unit // share

    def send_pair(c, q):
        return remote(
            terms.at[c, (1 - lo) * nrep + q], pair_in.at[c, q], d0s.at[c, q], d0r.at[c, q], partner
        )

    def send_plane(c, e):
        return remote(
            summed.at[c, e - 1], plane_in.at[c, e - 1], d1s.at[c, e - 1], d1r.at[c, e - 1],
            (xor(hi, e, half) * PAIR + lo, rep),
        )

    def to_owner(c):
        return remote(back.at[c], back_in.at[c], d2s.at[c], d2r.at[c], owner)

    def straight_to(n, q):
        f0, fs = tail[n]
        return remote(
            straight.at[q, pl.ds(f0, fs)], straight_in.at[hi, pl.ds(f0, fs)],
            d3s.at[n, q], d3r.at[n, hi], (rep * PAIR + lo, q),
        )

    def straight_from(n, k):
        f0, fs = tail[n]
        at = straight_in.at[k, pl.ds(f0, fs)]
        return remote(at, at, d3s.at[n, k], d3r.at[n, k], (k * PAIR + lo, hi))

    def send_late_pair(n, q):
        f0, fs = tail[n]
        return remote(
            terms.at[last, (1 - lo) * nrep + q, pl.ds(f0, fs)], pair_in.at[last, q, pl.ds(f0, fs)],
            t0s.at[n, q], t0r.at[n, q], partner,
        )

    def gain(sums, f0, fs, left, k, start, emit):
        for j in (1 - lo, lo):
            slot = 0 if j is lo else 1
            for u in range(rows // unit):
                a = adj[j, pl.ds(pl.multiple_of(k * share, share), share), u * unit : (u + 1) * unit]
                t = jnp.dot(left, a, preferred_element_type=F32)
                if not start:
                    t = t + sums[slot, u, f0 : f0 + fs, :]
                if emit is None:
                    sums[slot, u, f0 : f0 + fs, :] = t
                    continue
                t = t.astype(BF16)
                for v in range(per_unit):
                    emit(j, u * per_unit + v, t[:, v * share : (v + 1) * share])

    def emit_early(j, q, value):
        terms[0, j * nrep + q] = value
        if j is not lo:
            send_pair(0, q).start()

    def emit_late(n):
        f0, fs = tail[n]

        def emit(j, q, value):
            terms[last, j * nrep + q, f0 : f0 + fs, :] = value
            if j is not lo:
                send_late_pair(n, q).start()

        return emit

    def make_own():
        gain(acc, 0, lanes, dagg[0, rep].T, rep, True, None)
        gain(late_acc, 0, lanes, late[rep], rep, True, None)

    def make_early():
        near = far[::-1]
        for k in near:
            for i in range(PARTS):
                get_dagg(0, k, i).wait_recv()
            gain(acc, 0, lanes, dagg[0, k].T, k, False, emit_early if k is near[-1] else None)

    def make_late(n):
        f0, fs = tail[n]
        near = far[::-1]
        for k in near:
            get_late(n, k).wait_recv()
            gain(late_acc, f0, fs, late[k, f0 : f0 + fs, :], k, False, emit_late(n) if k is near[-1] else None)

    def send_late_plane(n, e):
        f0, fs = tail[n]
        at = (last, e - 1, pl.ds(f0, fs))
        return remote(
            summed.at[at], plane_in.at[at], t1s.at[n, e - 1], t1r.at[n, e - 1],
            (xor(hi, e, half) * PAIR + lo, rep),
        )

    def late_to_owner(n):
        f0, fs = tail[n]
        at = (last, pl.ds(f0, fs))
        return remote(back.at[at], back_in.at[at], t2s.at[n], t2r.at[n], owner)

    def add_late_plane(n):
        f0, fs = tail[n]
        both = back_sum[n + 1]
        for e in range(1, half):
            send_late_plane(n, e).wait_recv()
            both = both + plane_in[last, e - 1, f0 : f0 + fs, :].astype(F32)
        back[last, f0 : f0 + fs, :] = both.astype(BF16)

        @pl.when(moves)
        def _():
            late_to_owner(n).start()

    def add_late_pair(n):
        f0, fs = tail[n]
        if n not in DIRECT:
            for e in list(range(half - 1, 0, -1)) + [0]:
                q = xor(xor(hi, e, half), mirror(rep, nrep), nrep)
                send_late_pair(n, q).wait_recv()
                both = terms[last, lo * nrep + q, f0 : f0 + fs, :].astype(F32)
                both = both + pair_in[last, q, f0 : f0 + fs, :].astype(F32)
                if e > 0:
                    summed[last, e - 1, f0 : f0 + fs, :] = both.astype(BF16)
                    send_late_plane(n, e).start()
                else:
                    back_sum[n + 1] = both
            return
        for q in far + [rep]:
            send_late_pair(n, q).wait_recv()
            both = terms[last, lo * nrep + q, f0 : f0 + fs, :].astype(F32)
            both = (both + pair_in[last, q, f0 : f0 + fs, :].astype(F32)).astype(BF16)
            straight[q, f0 : f0 + fs, :] = both
            if q is rep:
                @pl.when(jnp.logical_not(is_src))
                def _():
                    straight_to(n, q).start()

                @pl.when(is_src)
                def _():
                    straight_in[hi, f0 : f0 + fs, :] = both
            else:
                straight_to(n, q).start()

    def add_pair(c):
        for e in list(range(half - 1, 0, -1)) + [0]:
            q = xor(xor(hi, e, half), mirror(rep, nrep), nrep)
            send_pair(c, q).wait_recv()
            both = terms[c, lo * nrep + q].astype(F32) + pair_in[c, q].astype(F32)
            if e > 0:
                summed[c, e - 1] = both.astype(BF16)
                send_plane(c, e).start()
            else:
                back_sum[c] = both

    def add_plane(c):
        both = back_sum[c]
        for e in range(1, half):
            send_plane(c, e).wait_recv()
            both = both + plane_in[c, e - 1].astype(F32)
        back[c] = both.astype(BF16)

        @pl.when(moves)
        def _():
            to_owner(c).start()

    back_sum = {}
    def send_w2(d):
        return remote(
            wrep_in.at[rep], wrep_in.at[rep], w2s.at[d - 1], w2r.at[d - 1], (row, (rep + d) % nrep)
        )

    def send_w3(e):
        return remote(
            wall.at[row], wall.at[row], w3s.at[e - 1], w3r.at[e - 1], (xor(hi, e, half) * PAIR + lo, rep)
        )

    def get_w3(e):
        at = wall.at[xor(hi, e, half) * PAIR + lo]
        return remote(at, at, w3s.at[e - 1], w3r.at[e - 1], (row, rep))

    def share_w3(e):
        at = wall.at[xor(hi, e, half) * PAIR + lo]
        return remote(at, at, w3ps.at[e], w3pr.at[e], partner)

    def shared_w3(e):
        at = wall.at[xor(hi, e, half) * PAIR + (1 - lo)]
        return remote(at, at, w3ps.at[e], w3pr.at[e], partner)

    def reduce_rows():
        wsum = wpart[row].astype(F32)
        for d in range(1, nrow):
            send_w1(d).wait_recv()
            wsum = wsum + wrow_in[d - 1].astype(F32)
        wrep_in[rep] = wsum.astype(BF16)
        for d in range(1, nrep):
            send_w2(d).start()

    def reduce_reps():
        for d in range(1, nrep):
            remote(
                wrep_in.at[rep], wrep_in.at[(rep + nrep - d) % nrep], w2s.at[d - 1], w2r.at[d - 1], (row, rep)
            ).wait_recv()
        wsum = wrep_in[0].astype(F32)
        for k in range(1, nrep):
            wsum = wsum + wrep_in[k].astype(F32)
        wall[row] = wsum.astype(BF16)
        for e in range(1, half):
            send_w3(e).start()
        share_w3(0).start()

    make_own()
    finish_sums()
    make_early()
    reduce_rows()
    add_pair(0)
    for n in range(len(tail)):
        make_late(n)
        add_late_pair(n)
    finish_gather()
    for c in range(last):
        add_plane(c)
    reduce_reps()
    for n in range(len(tail)):
        if n not in DIRECT:
            add_late_plane(n)
    for e in range(1, half):
        get_w3(e).wait_recv()
        share_w3(e).start()

    for c in range(last):
        cols = slice(c * lanes, (c + 1) * lanes)

        @pl.when(moves)
        def _():
            to_owner(c).wait_recv()
            gfeat[:, cols] = (base[:, cols] + back_in[c].astype(F32).T).astype(BF16)

        @pl.when(jnp.logical_not(moves))
        def _():
            gfeat[:, cols] = (base[:, cols] + back[c].astype(F32).T).astype(BF16)

    for n, (f0, fs) in enumerate(tail):
        if n not in DIRECT:
            cols = slice(last * lanes + f0, last * lanes + f0 + fs)

            @pl.when(moves)
            def _():
                late_to_owner(n).wait_recv()
                gfeat[:, cols] = (base[:, cols] + back_in[last, f0 : f0 + fs, :].astype(F32).T).astype(BF16)

            @pl.when(jnp.logical_not(moves))
            def _():
                gfeat[:, cols] = (base[:, cols] + back[last, f0 : f0 + fs, :].astype(F32).T).astype(BF16)

            continue
        for k in range(half):
            @pl.when(jnp.logical_or(rep != hi, hi != k))
            def _():
                straight_from(n, k).wait_recv()

        both = jnp.zeros((fs, share), F32)
        for k in range(half):
            both = both + straight_in[k, f0 : f0 + fs, :].astype(F32)
        both = both.astype(BF16).astype(F32)
        at = last * lanes + f0
        gfeat[:, at : at + fs] = (base[:, at : at + fs] + both.T).astype(BF16)
    for e in range(half):
        shared_w3(e).wait_recv()
    finish_rest()


def close_kernel(out_in, wall, gfeat_in, out, gself, gneigh, gfeat):
    half = wall.shape[0] // 2
    out[...] = out_in[...]
    gfeat[...] = gfeat_in[...]
    gself[...] = wall[pl.ds(0, half)].reshape(gself.shape).astype(F32)
    gneigh[...] = wall[pl.ds(half, half)].reshape(gneigh.shape).astype(F32)


def body(
    nrow, nrep,
    features, weight_self, weight_neigh, degrees, tile_values, tile_blocks, tile_count, cotangent,
):
    rows, width = features.shape
    here, slots, tile = tile_values.shape[1], tile_values.shape[2], tile_values.shape[-1]
    share = rows // nrep
    half = nrow // PAIR
    ny = half // PAIR
    piece = 2 * width // nrow
    lanes = 128
    slices = width // lanes
    pieces = nrep * SPLIT
    unit = max(share, 128)
    nt = len(TAIL)
    assert slices == 2 and here == PAIR and half == nrep and (rows // tile) ** 2 <= 128 and slots <= 128
    sems = pltpu.SemaphoreType.DMA
    vmem = pl.BlockSpec(memory_space=pltpu.VMEM)
    anywhere = pl.BlockSpec(memory_space=pltpu.HBM)

    def buf(*shape):
        return pltpu.VMEM(shape, BF16)

    out, wall, gfeat = pl.pallas_call(
        functools.partial(layer_kernel, nrow, nrep, here),
        out_shape=(
            jax.ShapeDtypeStruct((share, width), BF16),
            jax.ShapeDtypeStruct((nrow, piece, width), BF16),
            jax.ShapeDtypeStruct((share, width), BF16),
        ),
        in_specs=[anywhere] * 8,
        out_specs=(vmem,) * 3,
        scratch_shapes=[
            buf(width, width), buf(width, width),
            pltpu.VMEM((rows // tile, tile), jnp.int32),
            buf(share, width),
            pltpu.VMEM((here, 2, slots), jnp.int32),
            pltpu.SMEM((here,), jnp.int32),
            buf(here, slots, tile, tile),
            pltpu.VMEM((slots + 1, tile, tile), F32),
            buf(here, rows, rows),
            pltpu.VMEM((8, 128), jnp.int32),
            pltpu.VMEM((8, 128), jnp.int32),
            pltpu.SMEM((8, 128), jnp.int32),
            buf(share, width),
            buf(slices, here * pieces, rows // pieces, lanes),
            pltpu.VMEM((slices, share, lanes), F32),
            buf(slices, nrep, share, lanes),
            buf(slices, nrep, share, lanes),
            buf(share, width),
            buf(share, width),
            buf(slices, nrep, share, lanes),
            buf(nrep, lanes, share),
            pltpu.VMEM((here, rows // unit, lanes, unit), F32),
            pltpu.VMEM((here, rows // unit, lanes, unit), F32),
            buf(slices, nrow, lanes, share),
            buf(slices, nrep, lanes, share),
            buf(slices, half - 1, lanes, share),
            buf(slices, half - 1, lanes, share),
            buf(slices, lanes, share),
            buf(slices, lanes, share),
            buf(nrep, lanes, share),
            buf(half, lanes, share),
            buf(nrow, piece, width),
            buf(nrow - 1, piece, width),
            buf(nrep, piece, width),
            pltpu.VMEM((share, width), F32),
            pltpu.VMEM((rows, tile), F32),
            sems((6,)), sems((here,)), sems, sems, sems((slices, pieces)),
            sems((slices, pieces, ny)), sems((slices, pieces)), sems((slices, pieces)), sems((slices, pieces)),
            sems((slices, nrep)), sems((slices, nrep)),
            sems((nrep, PARTS)), sems((nrep, PARTS)),
            sems((slices, nrep, PARTS)), sems((slices, nrep, PARTS)),
            sems((nrow - 1,)), sems((nrow - 1,)),
            sems((nrep - 1,)), sems((nrep - 1,)),
            sems((half - 1,)), sems((half - 1,)), sems((half,)), sems((half,)),
            sems((slices, nrep)), sems((slices, nrep)),
            sems((slices, half - 1)), sems((slices, half - 1)),
            sems((slices,)), sems((slices,)),
            sems((nt, nrep)), sems((nt, half)), sems((nt, nrep)), sems((nt, nrep)),
            sems((nt, nrep)), sems((nt, nrep)),
            sems((nt, half - 1)), sems((nt, half - 1)), sems((nt,)), sems((nt,)),
        ],
        compiler_params=pltpu.CompilerParams(
            collective_id=0, has_side_effects=True, vmem_limit_bytes=44 * 2**20
        ),
        name="layer",
    )(*(
        pltpu.with_memory_space_constraint(x, pltpu.HBM)
        for x in (
            features, weight_self, weight_neigh, degrees.reshape(rows // tile, tile), cotangent,
            tile_values[0], tile_blocks.transpose(0, 1, 3, 2)[0], tile_count[0],
        )
    ))
    out, grad_self, grad_neigh, gfeat = pl.pallas_call(
        close_kernel,
        out_shape=(
            jax.ShapeDtypeStruct((share, width), BF16),
            jax.ShapeDtypeStruct((width, width), F32),
            jax.ShapeDtypeStruct((width, width), F32),
            jax.ShapeDtypeStruct((share, width), BF16),
        ),
        in_specs=[vmem] * 3,
        out_specs=(vmem,) * 4,
        compiler_params=pltpu.CompilerParams(vmem_limit_bytes=8 * 2**20),
        name="close",
    )(out, wall, gfeat)
    return out, grad_self, grad_neigh, gfeat


def solution(mesh):
    in_specs = (
        P("row", None),
        P(),
        P(),
        P("row"),
        P("row", "rep", None, None, None),
        P("row", "rep", None, None),
        P("row", "rep"),
        P(("row", "rep"), None),
    )
    out_specs = (P(("row", "rep"), None), P(), P(), P(("row", "rep"), None))
    run = functools.partial(body, mesh.shape["row"], mesh.shape["rep"])
    return jax.shard_map(run, mesh=mesh, in_specs=in_specs, out_specs=out_specs, check_vma=False)
```
